32 devices in a mesh: patch: 8 (over z, x), chan: 4 (over y, core).
Axes of the slice: x: 2, y: 2, z: 4, core: 2. Of those that a mesh axis runs over, the one named last changes fastest.
Arguments:
- grid_latent: bfloat16 [2048, 512], P('patch', 'chan'), may hold values from -6 to 6
- mesh_latent: bfloat16 [512, 512], P('patch', 'chan'), may hold values from -6 to 6
- w_source: bfloat16 [512, 512], replicated, may hold values from -0.25 to 0.25
- w_dest: bfloat16 [512, 512], replicated, may hold values from -0.25 to 0.25
- w_out: bfloat16 [512, 512], replicated, may hold values from -0.25 to 0.25
- edge_bias: float32 [512], P('chan'), may hold values from -3 to 3
- norm_gain: float32 [512], P('chan'), may hold values from 0.5 to 1.5
- edge_source: int32 [4096], P('patch'), may hold values from 0 to 255
- edge_patch: int32 [4096, 1], P('patch'), may hold values from 0 to 7; in each aligned block of 512 rows (0 to 511, 512 to 1023, ...) at most 128 rows name the same one
- edge_node: int32 [4096], P('patch'), may hold values from 0 to 63
- cotangent: bfloat16 [512, 512], P('patch', 'chan'), may hold values from -6 to 6
Outputs:
- updated: bfloat16 [512, 512], P('patch', 'chan')
- grad_grid: bfloat16 [2048, 512], P('patch', 'chan')
- grad_mesh: bfloat16 [512, 512], P('patch', 'chan')
- grad_w_source: float32 [512, 512], P(None, 'chan')
- grad_w_dest: float32 [512, 512], P(None, 'chan')
- grad_w_out: float32 [512, 512], P(None, 'chan')
- grad_bias: float32 [512], P('chan')
- grad_gain: float32 [512], P('chan')
The draws below stay inside these ranges and needn't reach their ends.
Inputs may be any that keep to these rules, and one draw needn't show every extreme that they name: `edge_patch`: the edges of band b are rows b * 512 to (b + 1) * 512 - 1; in the rows of one band no patch is named by more than 128 edges, and one patch is named by exactly 128.
All inputs are finite; a program needn't handle non-finite values.
Results may differ from the reference program's by a relative error of at most 0.0095.
Values may be sent and summed in bfloat16 or wider, within the bound.
A program may use at most 64 MiB of HBM per device.

```python
import math
import jax
import jax.numpy as jnp
import numpy as np
from jax import lax

LATENT = 512
GRID_DEV = 256
EDGE_DEV = 512
MESH_DEV = 64
CAP = 128
GRID_NODES = 2048
MESH_NODES = 512
EDGES = 4096
N_PATCH = 8


def place_ends(result, stream_key, least, top_value):
    dims = result.shape
    index_at = [jax.random.randint(jax.random.fold_in(stream_key, axis), (), 0, dims[axis]) for axis in range(len(dims))]
    result = result.at[tuple(index_at)].set(least)
    longest = dims.index(max(dims))
    index_at[longest] = (index_at[longest] + 1) % dims[longest]
    return result.at[tuple(index_at)].set(top_value)


def level_of(key, shape, shards, least, largest):
    factor_of, own = 1.0, jax.random.fold_in(key, 6)
    for position, shards_of in shards:
        draws = jnp.exp(jax.random.uniform(jax.random.fold_in(own, position), (shards_of,), jnp.float32, least / len(shards), largest / len(shards)))
        factor_of = factor_of * jnp.repeat(draws, shape[position] // shards_of).reshape([-1 if axis == position else 1 for axis in range(len(shape))])
    return factor_of


def shared_out(key, own, number, rows, number_of, top, most, skew):
    ranking = jax.random.permutation(key, number_of)
    crowded, usual = shares(number_of, rows * top, most, skew, True), shares(number_of, rows * top, most, skew, False)
    places = jnp.arange(number_of)

    def named(tallies, offset_by):
        used = int((tallies > 0).sum())
        fixed = max(1, used // 4)
        shifted = fixed + (places - fixed + offset_by * (used - fixed)) % max(1, number_of - fixed)
        return jnp.zeros((number_of,), jnp.int32).at[ranking[jnp.where(places < fixed, places, shifted)]].set(jnp.asarray(tallies, jnp.int32))

    tallies = jnp.where(number % 4 == 0, named(crowded, number // 4), named(usual, number - number // 4 - 1))
    mixed = jax.random.permutation(jax.random.fold_in(own, 3), number_of)
    donor, taker = mixed[0:number_of // 2 * 2:2], mixed[1:number_of // 2 * 2:2]
    margin = jnp.minimum(tallies[donor] - 1, most - tallies[taker]) // 2
    margin = jnp.where((donor == ranking[0]) | (taker == ranking[0]) | (tallies[taker] == 0), 0, jnp.maximum(margin, 0))
    shifted = jax.random.randint(jax.random.fold_in(own, 4), (number_of // 2,), 0, 1 << 20) % (margin + 1)
    tallies = tallies.at[donor].add(-shifted).at[taker].add(shifted)
    labels = jnp.searchsorted(jnp.cumsum(tallies), jnp.arange(rows * top), side="right").astype(jnp.int32)
    listing = labels.reshape(top, rows).T
    listing = listing[jax.random.permutation(jax.random.fold_in(own, 1), rows)]
    offset_by = jax.random.randint(jax.random.fold_in(own, 2), (rows, 1), 0, top)
    return jnp.take_along_axis(listing, (jnp.arange(top)[None, :] + offset_by) % top, axis=1)


def shares(amount, total, limit, slope, full):
    loads = [(1 << 20) // math.isqrt(rank ** slope) + 1 for rank in range(1, amount + 1)]
    largest = limit if full else min(limit, max(-(-total // amount), total * loads[0] // sum(loads)))
    least = 1 if total - largest >= amount - 1 else 0
    holding, spare = [largest] + [least] * (amount - 1), total - largest - least * (amount - 1)
    while spare > 0:
        free = [i for i in range(1, amount) if holding[i] < largest] or [i for i in range(1, amount) if holding[i] < limit]
        mass, remaining = sum([loads[i] for i in free]), spare
        for i in free:
            extra = min(limit - holding[i], max(1, remaining * loads[i] // mass), spare)
            holding[i] = holding[i] + extra
            spare = spare - extra
    return np.array(holding)


def gaussian(rng, dims, width, limit, split=(), kind=jnp.bfloat16):
    factor_of = level_of(rng, dims, split, -0.22, 0.18) if split else 1.0
    result = jax.random.normal(rng, dims, jnp.float32) * width * factor_of
    return jnp.minimum(jnp.maximum(result, -limit), limit).astype(kind)


def setup_inputs(seed: int = 0) -> dict:
    streams_of = jax.random.split(jax.random.key(seed), 12)
    grid_latent = gaussian(streams_of[0], (GRID_NODES, LATENT), 1.0, 6.0, ((0, 8), (1, 4)))
    mesh_latent = gaussian(streams_of[1], (MESH_NODES, LATENT), 1.0, 6.0, ((0, 8), (1, 4)))
    w_source = gaussian(streams_of[2], (LATENT, LATENT), LATENT ** -0.5, 0.25)
    w_dest = gaussian(streams_of[3], (LATENT, LATENT), LATENT ** -0.5, 0.25)
    w_out = gaussian(streams_of[4], (LATENT, LATENT), LATENT ** -0.5, 0.25)
    edge_bias = gaussian(streams_of[5], (LATENT,), 0.5, 3.0, ((0, 4),), jnp.float32)
    norm_gain = jnp.clip(1.0 + 0.1 * jax.random.normal(streams_of[6], (LATENT,), jnp.float32), 0.5, 1.5)
    edge_source = place_ends(jax.random.randint(streams_of[7], (EDGES,), 0, GRID_DEV), jax.random.fold_in(streams_of[7], 1), 0, GRID_DEV - 1).astype(jnp.int32)
    edge_patch_keys = jax.random.split(jax.random.fold_in(streams_of[8], 1), EDGES // EDGE_DEV)
    edge_patch_turns = jax.random.permutation(jax.random.fold_in(streams_of[8], 3), EDGES // EDGE_DEV)
    edge_patch = jax.vmap(lambda own, number: shared_out(jax.random.fold_in(streams_of[8], 2), own, number, EDGE_DEV, N_PATCH, 1, CAP, 2))(edge_patch_keys, edge_patch_turns).reshape((EDGES, 1))
    edge_node = place_ends(jax.random.randint(streams_of[9], (EDGES,), 0, MESH_DEV), jax.random.fold_in(streams_of[9], 1), 0, MESH_DEV - 1).astype(jnp.int32)
    cotangent = gaussian(streams_of[10], (MESH_NODES, LATENT), 1.0, 6.0, ((0, 8), (1, 4)))
    return dict(grid_latent=grid_latent, mesh_latent=mesh_latent, w_source=w_source, w_dest=w_dest, w_out=w_out, edge_bias=edge_bias, norm_gain=norm_gain, edge_source=edge_source, edge_patch=edge_patch, edge_node=edge_node, cotangent=cotangent)


norm_eps = 1e-05

def reference(grid_latent, mesh_latent, w_source, w_dest, w_out, edge_bias, norm_gain, edge_source, edge_patch, edge_node, cotangent):
    edge_total = edge_source.shape[0]
    band_index = (jnp.arange(edge_total, dtype=jnp.int32) // EDGE_DEV).astype(jnp.int32)
    src_row = (band_index * GRID_DEV + edge_source).astype(jnp.int32)
    dst_row = (edge_patch[:, 0] * MESH_DEV + edge_node).astype(jnp.int32)
    projected = jnp.dot(grid_latent, w_source, preferred_element_type=jnp.float32).astype(jnp.bfloat16)
    mesh_proj = jnp.dot(mesh_latent, w_dest, preferred_element_type=jnp.float32)
    pre_act = projected[src_row].astype(jnp.float32) + mesh_proj[dst_row] + edge_bias
    summed = jax.ops.segment_sum(jax.nn.silu(pre_act), dst_row, num_segments=MESH_NODES).astype(jnp.bfloat16)
    mixed = jnp.dot(summed, w_out, preferred_element_type=jnp.float32)
    row_mean = lax.optimization_barrier(jnp.mean(mixed, axis=1, keepdims=True))
    row_var = lax.optimization_barrier(jnp.mean(jnp.square(mixed - row_mean), axis=1, keepdims=True))
    inv_scale = lax.rsqrt(row_var + norm_eps)
    normed = (mixed - row_mean) * inv_scale
    updated = (mesh_latent.astype(jnp.float32) + normed * norm_gain).astype(jnp.bfloat16)
    cotan_full = cotangent.astype(jnp.float32)
    grad_gain = lax.optimization_barrier(jnp.sum(cotan_full * normed, axis=0))
    scaled = cotan_full * norm_gain
    grad_mixed = ((scaled - lax.optimization_barrier(jnp.mean(scaled, axis=1, keepdims=True)) - normed * lax.optimization_barrier(jnp.mean(scaled * normed, axis=1, keepdims=True))) * inv_scale).astype(jnp.bfloat16)
    grad_w_out = jnp.dot(summed.T, grad_mixed, preferred_element_type=jnp.float32)
    grad_summed = jnp.dot(grad_mixed, w_out.T, preferred_element_type=jnp.float32)
    sigmoid_val = jax.nn.sigmoid(pre_act)
    silu_slope = sigmoid_val * (1.0 + pre_act * (1.0 - sigmoid_val))
    grad_pre = (grad_summed[dst_row] * silu_slope).astype(jnp.bfloat16)
    grad_edges = grad_pre.astype(jnp.float32)
    grad_bias = lax.optimization_barrier(jnp.sum(grad_edges, axis=0))
    grad_mesh_proj = jax.ops.segment_sum(grad_edges, dst_row, num_segments=MESH_NODES).astype(jnp.bfloat16)
    grad_w_dest = jnp.dot(mesh_latent.T, grad_mesh_proj, preferred_element_type=jnp.float32)
    grad_mesh = (cotan_full + jnp.dot(grad_mesh_proj, w_dest.T, preferred_element_type=jnp.float32)).astype(jnp.bfloat16)
    grad_projected = jax.ops.segment_sum(grad_edges, src_row, num_segments=GRID_NODES).astype(jnp.bfloat16)
    grad_w_source = jnp.dot(grid_latent.T, grad_projected, preferred_element_type=jnp.float32)
    grad_grid = jnp.dot(grad_projected, w_source.T, preferred_element_type=jnp.float32).astype(jnp.bfloat16)
    return (updated, grad_grid, grad_mesh, grad_w_source, grad_w_dest, grad_w_out, grad_bias, grad_gain)
```

```python
import functools
import math

import jax
import jax.numpy as jnp
from jax import lax
from jax.experimental import pallas as pl
from jax.experimental.pallas import tpu as pltpu
from jax.sharding import PartitionSpec as P

norm_eps = 1e-05


def slot_ranks(dest_patch, patches):
    edge_count = dest_patch.shape[0]
    block_width = math.gcd(edge_count, 128)
    onehot = (
        dest_patch.reshape(edge_count // block_width, block_width)[:, :, None]
        == jnp.arange(patches, dtype=jnp.int32)[None, None, :]
    ).astype(jnp.float32)
    strict_lower = (jnp.arange(block_width)[:, None] > jnp.arange(block_width)[None, :]).astype(
        jnp.float32
    )
    within = jnp.einsum("ij,bjp->bip", strict_lower, onehot, precision=lax.Precision.HIGHEST)
    counts = jnp.sum(onehot, axis=1)
    blocks = jnp.arange(counts.shape[0])
    earlier = (blocks[:, None] > blocks[None, :]).astype(jnp.float32)
    before = jnp.dot(earlier, counts, precision=lax.Precision.HIGHEST)
    position = jnp.sum((within + before[:, None, :]) * onehot, axis=2)
    return position.reshape(edge_count).astype(jnp.int32)


def contract_rows(left, right):
    return lax.dot_general(
        left, right, (((0,), (0,)), ((), ())), preferred_element_type=jnp.float32
    )


def contract_cols(left, right):
    return lax.dot_general(
        left, right, (((1,), (1,)), ((), ())), preferred_element_type=jnp.float32
    )


def on_device(
    grid_latent,
    mesh_latent,
    w_source,
    w_dest,
    w_out,
    edge_bias,
    norm_gain,
    edge_source,
    edge_patch,
    edge_node,
    cotangent,
):
    patches = lax.axis_size("patch")
    slice_width = grid_latent.shape[1]
    latent_width = w_source.shape[0]
    offset = lax.axis_index("chan") * slice_width
    grid_count = grid_latent.shape[0]
    mesh_count = mesh_latent.shape[0]
    edge_count = edge_source.shape[0]
    capacity = max(2, 2 * edge_count // patches)
    slots = patches * capacity
    dest_patch = edge_patch[:, 0]
    slot_index = dest_patch * capacity + slot_ranks(dest_patch, patches)
    grid_full = lax.all_gather(grid_latent, "chan", axis=1, tiled=True)
    mesh_full = lax.all_gather(mesh_latent, "chan", axis=1, tiled=True)
    source_cols = lax.dynamic_slice_in_dim(w_source, offset, slice_width, 1)
    dest_cols = lax.dynamic_slice_in_dim(w_dest, offset, slice_width, 1)
    out_cols = lax.dynamic_slice_in_dim(w_out, offset, slice_width, 1)
    mesh_proj = jnp.dot(mesh_full, dest_cols, preferred_element_type=jnp.float32)
    empty_rows = jnp.zeros((slots, slice_width), jnp.bfloat16)
    projected = jnp.dot(grid_full, source_cols, preferred_element_type=jnp.float32).astype(
        jnp.bfloat16
    )
    outgoing = empty_rows.at[slot_index].set(projected[edge_source])
    targets = jnp.full((slots,), mesh_count, jnp.int32).at[slot_index].set(edge_node)
    arrived = lax.all_to_all(
        outgoing.reshape(patches, capacity, slice_width),
        "patch",
        split_axis=0,
        concat_axis=0,
        tiled=True,
    )
    landed = lax.all_to_all(
        targets.reshape(patches, capacity), "patch", split_axis=0, concat_axis=0, tiled=True
    )
    edge_values = arrived.reshape(slots, slice_width)
    landed = landed.reshape(slots)
    is_live = landed < mesh_count
    safe_node = jnp.minimum(landed, mesh_count - 1)
    pre_act = edge_values.astype(jnp.float32) + mesh_proj[safe_node] + edge_bias
    message = jnp.where(is_live[:, None], jax.nn.silu(pre_act), 0.0)
    summed = jax.ops.segment_sum(message, safe_node, num_segments=mesh_count).astype(jnp.bfloat16)
    summed_full = lax.all_gather(summed, "chan", axis=1, tiled=True)
    mixed = jnp.dot(summed_full, out_cols, preferred_element_type=jnp.float32)
    row_total, row_square = lax.psum(
        (jnp.sum(mixed, axis=1), jnp.sum(mixed * mixed, axis=1)), "chan"
    )
    row_mean = row_total / latent_width
    row_var = jnp.maximum(row_square / latent_width - row_mean * row_mean, 0.0)
    inv_scale = lax.rsqrt(row_var + norm_eps)
    normed = (mixed - row_mean[:, None]) * inv_scale[:, None]
    updated = (mesh_latent.astype(jnp.float32) + normed * norm_gain).astype(jnp.bfloat16)
    cotan_full = cotangent.astype(jnp.float32)
    gain_local = jnp.sum(cotan_full * normed, axis=0)
    scaled = cotan_full * norm_gain
    scaled_total, cross_total = lax.psum(
        (jnp.sum(scaled, axis=1), jnp.sum(scaled * normed, axis=1)), "chan"
    )
    grad_mixed = (
        (
            scaled
            - scaled_total[:, None] / latent_width
            - normed * (cross_total[:, None] / latent_width)
        )
        * inv_scale[:, None]
    ).astype(jnp.bfloat16)
    out_local = contract_rows(summed_full, grad_mixed)
    grad_full = lax.all_gather(grad_mixed, "chan", axis=1, tiled=True)
    grad_summed = contract_cols(grad_full, lax.dynamic_slice_in_dim(w_out, offset, slice_width, 0))
    sigmoid_val = jax.nn.sigmoid(pre_act)
    silu_slope = sigmoid_val * (1.0 + pre_act * (1.0 - sigmoid_val))
    grad_pre = jnp.where(is_live[:, None], grad_summed[safe_node] * silu_slope, 0.0).astype(
        jnp.bfloat16
    )
    grad_edges = grad_pre.astype(jnp.float32)
    bias_local = jnp.sum(grad_edges, axis=0)
    grad_mesh_proj = jax.ops.segment_sum(grad_edges, safe_node, num_segments=mesh_count).astype(
        jnp.bfloat16
    )
    returned = lax.all_to_all(
        grad_pre.reshape(patches, capacity, slice_width),
        "patch",
        split_axis=0,
        concat_axis=0,
        tiled=True,
    )
    per_edge = returned.reshape(slots, slice_width)[slot_index]
    grad_projected = jax.ops.segment_sum(
        per_edge.astype(jnp.float32), edge_source, num_segments=grid_count
    ).astype(jnp.bfloat16)
    dest_local = contract_rows(mesh_full, grad_mesh_proj)
    source_local = contract_rows(grid_full, grad_projected)
    node_full = lax.all_gather(grad_mesh_proj, "chan", axis=1, tiled=True)
    grad_mesh = (
        cotan_full
        + contract_cols(node_full, lax.dynamic_slice_in_dim(w_dest, offset, slice_width, 0))
    ).astype(jnp.bfloat16)
    source_full = lax.all_gather(grad_projected, "chan", axis=1, tiled=True)
    grad_grid = contract_cols(
        source_full, lax.dynamic_slice_in_dim(w_source, offset, slice_width, 0)
    ).astype(jnp.bfloat16)
    grad_w_source, grad_w_dest, grad_w_out, grad_bias, grad_gain = lax.psum(
        (source_local, dest_local, out_local, bias_local, gain_local), "patch"
    )
    return (
        updated,
        grad_grid,
        grad_mesh,
        grad_w_source,
        grad_w_dest,
        grad_w_out,
        grad_bias,
        grad_gain,
    )


MESH = pl.DeviceIdType.MESH
f32, bf16 = jnp.float32, jnp.bfloat16


def fused_kernel(
    P_, C_, B_,
    grid_hbm, mesh_hbm, cot_hbm, bias_hbm, gain_hbm, src_hbm, patch_hbm, node_hbm,
    ws_hbm, wd_hbm, wo_hbm,
    upd_ref, ggrid_ref, gmesh_ref, gws_ref, gwd_ref, gwo_ref, gbias_ref, ggain_ref,
    ws_col, ws_row, wd_col, wd_row, wo,
    gridz, meshb, cotb, gainb, bias_ref, gain_ref, ends,
    mp, ps, pr, qs, qr, qn, sm, nrm, gm, gs, gmn, gp, gmp, ns, nt,
    ends_h, src_t, dst_t, slope, grid_t, gpz, wsend, wrecv, bsend, brecv,
    w_sem, c_send, c_recv, p_send, p_recv, z_send, z_recv, s_send, s_recv, x_send, x_recv,
):
    me_p, me_c = lax.axis_index("patch"), lax.axis_index("chan")
    G, W = grid_hbm.shape
    M = mesh_hbm.shape[0]
    L = C_ * W
    E = src_hbm.shape[1]
    N = P_ * M
    H_ = P_ // B_
    lo, hi = lax.rem(me_p, B_), me_p // B_
    started = []

    barrier = pltpu.get_barrier_semaphore()
    for k in range(1, P_):
        pl.semaphore_signal(barrier, inc=1, device_id=(lax.rem(me_p + k, P_), me_c), device_id_type=MESH)
    for j in range(1, C_):
        pl.semaphore_signal(barrier, inc=1, device_id=(me_p, lax.rem(me_c + j, C_)), device_id_type=MESH)

    cols = pl.ds(pl.multiple_of(me_c * W, W), W)
    fills = [
        pltpu.make_async_copy(src, dst, w_sem.at[5 + i]) for i, (src, dst) in enumerate((
            (mesh_hbm, meshb.at[me_c]), (grid_hbm, gridz.at[me_c, 0]), (cot_hbm, cotb.at[me_c]),
            (gain_hbm, gain_ref), (bias_hbm, bias_ref), (src_hbm, ends.at[0, :, pl.ds(0, E)]),
            (patch_hbm, ends.at[0, :, pl.ds(E, E)]), (node_hbm, ends.at[0, :, pl.ds(2 * E, E)])))]
    loads = [
        pltpu.make_async_copy(wd_hbm.at[:, cols], wd_col, w_sem.at[0]),
        pltpu.make_async_copy(ws_hbm.at[:, cols], ws_col, w_sem.at[1]),
        pltpu.make_async_copy(wo_hbm, wo, w_sem.at[2]),
        pltpu.make_async_copy(wd_hbm.at[cols, :], wd_row, w_sem.at[3]),
        pltpu.make_async_copy(ws_hbm.at[cols, :], ws_row, w_sem.at[4]),
    ]
    for load in fills + loads:
        load.start()

    def remote(src, dst, send_sem, recv_sem, to):
        copy = pltpu.make_async_remote_copy(
            src_ref=src, dst_ref=dst, send_sem=send_sem, recv_sem=recv_sem,
            device_id=to, device_id_type=MESH)
        copy.start()
        started.append(copy)
        return copy

    def chan_gather(phase, src, buf):
        return [
            remote(src, buf.at[me_c], c_send.at[phase, j], c_recv.at[phase, j],
                   (me_p, lax.rem(me_c + j, C_)))
            for j in range(1, C_)]

    def patch_gather(phase, src, slot):
        return [
            remote(src, slot(k), p_send.at[phase, k], p_recv.at[phase, k],
                   (lax.rem(me_p + k, P_), me_c))
            for k in range(1, P_)]

    def patch_scatter(phase, block, buf):
        return [
            remote(block(k), buf.at[k], p_send.at[phase, k], p_recv.at[phase, k],
                   (lax.rem(me_p + P_ - k, P_), me_c))
            for k in range(1, P_)]

    def line_gather(phase, slot):
        return [
            remote(slot(0), slot(h), z_send.at[phase, h], z_recv.at[phase, h],
                   (lax.rem(me_p + h * B_, P_), me_c))
            for h in range(1, H_)]

    even = C_ % 2 == 0
    twin = me_c + 1 - 2 * lax.rem(me_c, 2)

    def spread(phase, view):
        if not even:
            return [], [
                remote(view(me_c), view(me_c), s_send.at[phase, j], s_recv.at[phase, j],
                       (me_p, lax.rem(me_c + j, C_)))
                for j in range(1, C_)]
        near = [remote(view(me_c), view(me_c), s_send.at[phase, 0], s_recv.at[phase, 0], (me_p, twin))]
        across = [
            remote(view(me_c), view(me_c), s_send.at[phase, j], s_recv.at[phase, j],
                   (me_p, lax.rem(me_c + 2 * j, C_)))
            for j in range(1, C_ // 2)]
        return near, across

    def spread_on(phase, view, across):
        arrived(across)
        if not even:
            return []
        passed = []
        for j in range(1, C_ // 2):
            block = view(lax.rem(me_c + C_ - 2 * j, C_))
            passed.append(remote(
                block, block, s_send.at[phase, C_ // 2 + j], s_recv.at[phase, C_ // 2 + j], (me_p, twin)))
        return passed

    def arrived(copies):
        for copy in copies:
            copy.wait_recv()

    def wide(buf):
        return jnp.concatenate([buf[c] for c in range(C_)], axis=1)

    def dot(a, b):
        return lax.dot_general(a, b, (((1,), (0,)), ((), ())), preferred_element_type=f32)

    def onehot_of(mask):
        return jnp.where(mask, 1.0, 0.0).astype(bf16)

    def flat(buf):
        return buf[...].reshape(N, W)

    def band_ends(h):
        row = ends[h]
        away = me_p - row[:, E:2 * E]
        away = jnp.where(away < 0, away + P_, away)
        return row[:, :E], away * M + row[:, 2 * E:]

    def band_onehots(h):
        src, dst = band_ends(h)
        down = jnp.transpose(jnp.broadcast_to(jnp.concatenate([src, dst], axis=1), (128, 2 * E)))
        lane = lax.broadcasted_iota(jnp.int32, (E, 128), 1)
        for b in range(0, G, 128):
            ends_h[h, :, b:b + 128] = onehot_of(down[:E] == lane + b)
        for b in range(0, N, 128):
            ends_h[h, :, G + b:G + b + 128] = onehot_of(down[E:] == lane + b)
        src_t[h] = onehot_of(lax.broadcasted_iota(jnp.int32, (G, E), 0) == src)

    def band_full(h):
        return jnp.concatenate([gridz[c, h] for c in range(C_)], axis=1)

    def sigmoid(pre):
        return 1.0 / (1.0 + jnp.exp(-pre))

    def silu_slope(pre, sig):
        return sig * (1.0 + pre * (1.0 - sig))

    fills[0].wait()
    pl.semaphore_wait(barrier, P_ + C_ - 2)
    mesh_in = chan_gather(0, meshb.at[me_c], meshb)
    for fill in fills[1:]:
        fill.wait()
    grid_in = chan_gather(1, gridz.at[me_c, 0], gridz.at[:, 0])
    ends_in = line_gather(1, lambda h: ends.at[h])
    line_in = line_gather(0, lambda h: gridz.at[me_c, h])
    gainb[me_c] = jnp.broadcast_to(gain_ref[...], gainb.shape[1:])
    ns[me_c, 0, 0] = meshb[me_c]

    loads[0].wait()
    arrived(mesh_in)
    mp[0] = (dot(wide(meshb), wd_col[...]) + bias_ref[...]).astype(bf16)
    mp_in = patch_gather(0, mp.at[0], lambda k: mp.at[k])
    cot_in = chan_gather(2, cotb.at[me_c], cotb)
    gain_in = chan_gather(3, gainb.at[me_c], gainb)

    band_onehots(0)
    dst_t[...] = onehot_of(lax.broadcasted_iota(jnp.int32, (N, E), 0) == band_ends(0)[1])
    loads[1].wait()
    arrived(grid_in)
    projected = dot(band_full(0), ws_col[...]).astype(bf16)
    sender = dot(ends_h[0, :, :G], projected)
    nodes_in = patch_gather(3, ns.at[me_c, 0, 0], lambda k: ns.at[me_c, 0, k])
    arrived(line_in)
    bands = lambda c: gridz.at[c, pl.ds(1, H_ - 1)]
    band_near, band_across = spread(0, bands)

    arrived(mp_in)
    pre = sender + dot(ends_h[0, :, G:], flat(mp))
    sig = sigmoid(pre)
    part = dot(dst_t[...], (pre * sig).astype(bf16))
    ps[...] = part.astype(bf16).reshape(P_, M, W)
    part_in = patch_scatter(1, lambda k: ps.at[k], pr)
    own_slope = silu_slope(pre, sig)
    slope[0] = own_slope
    turned = dot(dst_t[...], own_slope.astype(bf16))
    qs[...] = turned.astype(bf16).reshape(P_, M, W)
    turned_in = patch_scatter(2, lambda k: qs.at[k], qr)
    total = part[:M]
    slope_total = turned[:M]

    arrived(ends_in)

    def other_onehots(h, carry):
        band_onehots(h)
        return carry

    lax.fori_loop(1, H_, other_onehots, 0)
    grid_t[:, 0:G] = jnp.transpose(band_full(0))
    band_passed = spread_on(0, bands, band_across)

    arrived(part_in)
    for k in range(1, P_):
        total = total + pr[k].astype(f32)
    sm[me_c] = total.astype(bf16)
    sm_in = chan_gather(4, sm.at[me_c], sm)
    ns[me_c, 1, 0] = total.astype(bf16)
    sums_in = patch_gather(4, sm.at[me_c], lambda k: ns.at[me_c, 1, k])
    arrived(turned_in)
    for k in range(1, P_):
        slope_total = slope_total + qr[k].astype(f32)
    qn[0] = slope_total.astype(bf16)
    qn_in = patch_gather(5, qn.at[0], lambda k: qn.at[k])

    loads[2].wait()
    arrived(cot_in)
    arrived(gain_in)
    gain_full = jnp.concatenate([gainb[c][0:1] for c in range(C_)], axis=1)
    scaled = wide(cotb).astype(f32) * gain_full
    scaled_mean = jnp.sum(scaled, axis=1, keepdims=True) / L
    arrived(sm_in)
    mixed = dot(wide(sm), wo[...])
    mean = jnp.sum(mixed, axis=1, keepdims=True) / L
    centred = mixed - mean
    var = jnp.sum(centred * centred, axis=1, keepdims=True) / L
    inv = lax.rsqrt(var + norm_eps)
    normed = centred * inv
    cross_mean = jnp.sum(scaled * normed, axis=1, keepdims=True) / L
    grad_mixed = ((scaled - scaled_mean - normed * cross_mean) * inv).astype(bf16)
    grad_summed = contract_cols(grad_mixed, wo[cols, :])
    gs[0] = grad_summed.astype(bf16)
    gs_in = patch_gather(6, gs.at[0], lambda k: gs.at[k])

    grad_nodes = grad_summed * slope_total
    gmp[me_c] = grad_nodes.astype(bf16)
    gmp_in = chan_gather(6, gmp.at[me_c], gmp)
    for c in range(C_):
        nrm[c] = normed[:, c * W:(c + 1) * W]
        gm[c] = grad_mixed[:, c * W:(c + 1) * W]
    gmn[0] = gm[me_c]
    gmn_in = patch_gather(7, gmn.at[0], lambda k: gmn.at[k])
    own_normed = nrm[me_c]
    cot_own = cotb[me_c].astype(f32)
    bsend[...] = jnp.concatenate(
        [jnp.sum(grad_nodes, axis=0, keepdims=True),
         jnp.sum(cot_own * own_normed, axis=0, keepdims=True), jnp.zeros((6, W), f32)], axis=0)
    small_in = patch_gather(8, bsend, lambda k: brecv.at[k])
    upd_ref[...] = (meshb[me_c].astype(f32) + own_normed * gain_ref[...]).astype(bf16)

    arrived(nodes_in)
    arrived(sums_in)
    rows = lambda c: ns.at[c]
    rows_near, rows_across = spread(1, rows)

    arrived(band_near)
    arrived(band_passed)

    def other_slopes(h, carry):
        full = band_full(h)
        grid_t[:, pl.ds(pl.multiple_of(h * G, G), G)] = jnp.transpose(full)
        pre = dot(ends_h[h, :, :G], dot(full, ws_col[...]).astype(bf16)) + dot(ends_h[h, :, G:], flat(mp))
        slope[h] = silu_slope(pre, sigmoid(pre))
        return carry

    lax.fori_loop(1, H_, other_slopes, 0)
    loads[3].wait()
    loads[4].wait()
    arrived(gmp_in)
    gmesh_ref[...] = (cot_own + contract_cols(wide(gmp), wd_row[...])).astype(bf16)

    def turn(c):
        for i in range(2):
            nt[c, i] = jnp.transpose(ns[c, i].reshape(N, W))

    turn(me_c)
    if even:
        arrived(rows_near)
        turn(twin)

    def band_grad(h):
        grad_pre = (dot(ends_h[h, :, G:], flat(gs)) * slope[h]).astype(bf16)
        return dot(src_t[h], grad_pre).astype(bf16)

    arrived(gs_in)
    grad_projected = band_grad(0)
    gp[me_c] = grad_projected
    gp_in = chan_gather(5, gp.at[me_c], gp)
    gpz[0:G] = grad_projected
    rows_passed = spread_on(1, rows, rows_across)
    for h in range(1, H_):
        gpz[h * G:(h + 1) * G] = band_grad(h)
    weight_in = []
    half = L // 2
    for i in range(2):
        piece = pl.ds(i * half, half)
        wsend[piece] = dot(grid_t[piece, :], gpz[...]).astype(bf16)
        weight_in += [
            remote(wsend.at[piece], wrecv.at[b, piece], x_send.at[i, b], x_recv.at[i, b],
                   (hi * B_ + lax.rem(lo + b, B_), me_c))
            for b in range(1, B_)]

    for j in range(1, C_ // 2 if even else C_):
        turn(lax.rem(me_c + C_ - (2 * j if even else j), C_))
    arrived(rows_passed)
    if even:
        for j in range(1, C_ // 2):
            turn(lax.rem(twin + C_ - 2 * j, C_))
    arrived(qn_in)
    grad_nodes_all = (flat(gs).astype(f32) * flat(qn).astype(f32)).astype(bf16)
    for c in range(C_):
        gwd_ref[c * W:(c + 1) * W, :] = dot(nt[c, 0], grad_nodes_all)
    arrived(gmn_in)
    for c in range(C_):
        gwo_ref[c * W:(c + 1) * W, :] = dot(nt[c, 1], flat(gmn))
    arrived(small_in)
    small = bsend[...]
    for k in range(1, P_):
        small = small + brecv[k]
    gbias_ref[...] = small[0:1]
    ggain_ref[...] = small[1:2]
    arrived(gp_in)
    ggrid_ref[...] = contract_cols(wide(gp), ws_row[...]).astype(bf16)
    arrived(weight_in)
    source = wsend[...].astype(f32)
    for b in range(1, B_):
        source = source + wrecv[b].astype(f32)
    gws_ref[...] = source
    for copy in started:
        copy.wait_send()


def write_out(*refs):
    sems = refs[-1]
    copies = [
        pltpu.make_async_copy(refs[i], refs[8 + i], sems.at[i]) for i in range(8)]
    for copy in copies:
        copy.start()
    for copy in copies:
        copy.wait()


def fused_on_device(
    patches, chans,
    grid_latent, mesh_latent, w_source, w_dest, w_out, edge_bias, norm_gain,
    edge_source, edge_patch, edge_node, cotangent,
):
    G, W = grid_latent.shape
    M = mesh_latent.shape[0]
    L = w_source.shape[0]
    E = edge_source.shape[0]
    N = patches * M
    near = 2 if patches % 2 == 0 else 1
    far = patches // near
    vmem = pl.BlockSpec(memory_space=pltpu.VMEM)
    hbm = pl.BlockSpec(memory_space=pltpu.HBM)
    sds = jax.ShapeDtypeStruct

    def buf(*shape, dtype=bf16):
        return pltpu.VMEM(shape, dtype)

    def sems(*shape):
        return [pltpu.SemaphoreType.DMA(shape), pltpu.SemaphoreType.DMA(shape)]

    nodes = buf(patches, M, W)
    outs = pl.pallas_call(
        functools.partial(fused_kernel, patches, chans, near),
        out_shape=(
            sds((M, W), bf16), sds((G, W), bf16), sds((M, W), bf16),
            sds((L, W), f32), sds((L, W), f32), sds((L, W), f32),
            sds((1, W), f32), sds((1, W), f32),
        ),
        in_specs=[hbm] * 11,
        out_specs=(vmem,) * 8,
        scratch_shapes=[
            buf(L, W), buf(W, L), buf(L, W), buf(W, L), buf(L, L),
            buf(chans, far, G, W), buf(chans, M, W), buf(chans, M, W), buf(chans, 8, W, dtype=f32),
            buf(1, W, dtype=f32), buf(1, W, dtype=f32), buf(far, 1, 3 * E, dtype=jnp.int32),
            nodes, nodes, nodes, nodes, nodes, nodes, buf(chans, M, W), buf(chans, M, W, dtype=f32),
            buf(chans, M, W), nodes, nodes, buf(chans, G, W), buf(chans, M, W),
            buf(chans, 2, patches, M, W), buf(chans, 2, W, N),
            buf(far, E, G + N), buf(far, G, E), buf(N, E), buf(far, E, W, dtype=f32),
            buf(L, far * G), buf(far * G, W), buf(L, W), buf(near, L, W),
            buf(8, W, dtype=f32), buf(patches, 8, W, dtype=f32),
            pltpu.SemaphoreType.DMA((13,)),
            *sems(7, chans), *sems(9, patches), *sems(2, far), *sems(2, chans + 1), *sems(2, near),
        ],
        compiler_params=pltpu.CompilerParams(
            collective_id=0, has_side_effects=True, vmem_limit_bytes=60 * 1024 * 1024),
    )(
        grid_latent, mesh_latent, cotangent, edge_bias.reshape(1, W), norm_gain.reshape(1, W),
        edge_source.reshape(1, E), edge_patch.reshape(1, E), edge_node.reshape(1, E),
        w_source, w_dest, w_out,
    )
    outs = pl.pallas_call(
        write_out,
        out_shape=tuple(sds(out.shape, out.dtype) for out in outs),
        in_specs=[vmem] * 8,
        out_specs=(hbm,) * 8,
        scratch_shapes=[pltpu.SemaphoreType.DMA((8,))],
    )(*outs)
    return outs[:6] + (outs[6].reshape(W), outs[7].reshape(W))


def device_program(mesh):
    patches, chans = mesh.shape["patch"], mesh.shape["chan"]
    if patches <= 16:
        return functools.partial(fused_on_device, patches, chans)
    return on_device


def solution(mesh):
    placed = (
        P("patch", "chan"),
        P("patch", "chan"),
        P(),
        P(),
        P(),
        P("chan"),
        P("chan"),
        P("patch"),
        P("patch", None),
        P("patch"),
        P("patch", "chan"),
    )
    return jax.shard_map(
        device_program(mesh),
        mesh=mesh,
        in_specs=placed,
        out_specs=(
            P("patch", "chan"),
            P("patch", "chan"),
            P("patch", "chan"),
            P(None, "chan"),
            P(None, "chan"),
            P(None, "chan"),
            P("chan"),
            P("chan"),
        ),
        check_vma=False,
    )
```

```python
import functools
import math

import jax
import jax.numpy as jnp
from jax import lax
from jax.experimental import pallas as pl
from jax.experimental.pallas import tpu as pltpu
from jax.sharding import PartitionSpec as P

norm_eps = 1e-05


def slot_ranks(dest_patch, patches):
    edge_count = dest_patch.shape[0]
    block_width = math.gcd(edge_count, 128)
    onehot = (
        dest_patch.reshape(edge_count // block_width, block_width)[:, :, None]
        == jnp.arange(patches, dtype=jnp.int32)[None, None, :]
    ).astype(jnp.float32)
    strict_lower = (jnp.arange(block_width)[:, None] > jnp.arange(block_width)[None, :]).astype(
        jnp.float32
    )
    within = jnp.einsum("ij,bjp->bip", strict_lower, onehot, precision=lax.Precision.HIGHEST)
    counts = jnp.sum(onehot, axis=1)
    blocks = jnp.arange(counts.shape[0])
    earlier = (blocks[:, None] > blocks[None, :]).astype(jnp.float32)
    before = jnp.dot(earlier, counts, precision=lax.Precision.HIGHEST)
    position = jnp.sum((within + before[:, None, :]) * onehot, axis=2)
    return position.reshape(edge_count).astype(jnp.int32)


def contract_rows(left, right):
    return lax.dot_general(
        left, right, (((0,), (0,)), ((), ())), preferred_element_type=jnp.float32
    )


def contract_cols(left, right):
    return lax.dot_general(
        left, right, (((1,), (1,)), ((), ())), preferred_element_type=jnp.float32
    )


def on_device(
    grid_latent,
    mesh_latent,
    w_source,
    w_dest,
    w_out,
    edge_bias,
    norm_gain,
    edge_source,
    edge_patch,
    edge_node,
    cotangent,
):
    patches = lax.axis_size("patch")
    slice_width = grid_latent.shape[1]
    latent_width = w_source.shape[0]
    offset = lax.axis_index("chan") * slice_width
    grid_count = grid_latent.shape[0]
    mesh_count = mesh_latent.shape[0]
    edge_count = edge_source.shape[0]
    capacity = max(2, 2 * edge_count // patches)
    slots = patches * capacity
    dest_patch = edge_patch[:, 0]
    slot_index = dest_patch * capacity + slot_ranks(dest_patch, patches)
    grid_full = lax.all_gather(grid_latent, "chan", axis=1, tiled=True)
    mesh_full = lax.all_gather(mesh_latent, "chan", axis=1, tiled=True)
    source_cols = lax.dynamic_slice_in_dim(w_source, offset, slice_width, 1)
    dest_cols = lax.dynamic_slice_in_dim(w_dest, offset, slice_width, 1)
    out_cols = lax.dynamic_slice_in_dim(w_out, offset, slice_width, 1)
    mesh_proj = jnp.dot(mesh_full, dest_cols, preferred_element_type=jnp.float32)
    empty_rows = jnp.zeros((slots, slice_width), jnp.bfloat16)
    projected = jnp.dot(grid_full, source_cols, preferred_element_type=jnp.float32).astype(
        jnp.bfloat16
    )
    outgoing = empty_rows.at[slot_index].set(projected[edge_source])
    targets = jnp.full((slots,), mesh_count, jnp.int32).at[slot_index].set(edge_node)
    arrived = lax.all_to_all(
        outgoing.reshape(patches, capacity, slice_width),
        "patch",
        split_axis=0,
        concat_axis=0,
        tiled=True,
    )
    landed = lax.all_to_all(
        targets.reshape(patches, capacity), "patch", split_axis=0, concat_axis=0, tiled=True
    )
    edge_values = arrived.reshape(slots, slice_width)
    landed = landed.reshape(slots)
    is_live = landed < mesh_count
    safe_node = jnp.minimum(landed, mesh_count - 1)
    pre_act = edge_values.astype(jnp.float32) + mesh_proj[safe_node] + edge_bias
    message = jnp.where(is_live[:, None], jax.nn.silu(pre_act), 0.0)
    summed = jax.ops.segment_sum(message, safe_node, num_segments=mesh_count).astype(jnp.bfloat16)
    summed_full = lax.all_gather(summed, "chan", axis=1, tiled=True)
    mixed = jnp.dot(summed_full, out_cols, preferred_element_type=jnp.float32)
    row_total, row_square = lax.psum(
        (jnp.sum(mixed, axis=1), jnp.sum(mixed * mixed, axis=1)), "chan"
    )
    row_mean = row_total / latent_width
    row_var = jnp.maximum(row_square / latent_width - row_mean * row_mean, 0.0)
    inv_scale = lax.rsqrt(row_var + norm_eps)
    normed = (mixed - row_mean[:, None]) * inv_scale[:, None]
    updated = (mesh_latent.astype(jnp.float32) + normed * norm_gain).astype(jnp.bfloat16)
    cotan_full = cotangent.astype(jnp.float32)
    gain_local = jnp.sum(cotan_full * normed, axis=0)
    scaled = cotan_full * norm_gain
    scaled_total, cross_total = lax.psum(
        (jnp.sum(scaled, axis=1), jnp.sum(scaled * normed, axis=1)), "chan"
    )
    grad_mixed = (
        (
            scaled
            - scaled_total[:, None] / latent_width
            - normed * (cross_total[:, None] / latent_width)
        )
        * inv_scale[:, None]
    ).astype(jnp.bfloat16)
    out_local = contract_rows(summed_full, grad_mixed)
    grad_full = lax.all_gather(grad_mixed, "chan", axis=1, tiled=True)
    grad_summed = contract_cols(grad_full, lax.dynamic_slice_in_dim(w_out, offset, slice_width, 0))
    sigmoid_val = jax.nn.sigmoid(pre_act)
    silu_slope = sigmoid_val * (1.0 + pre_act * (1.0 - sigmoid_val))
    grad_pre = jnp.where(is_live[:, None], grad_summed[safe_node] * silu_slope, 0.0).astype(
        jnp.bfloat16
    )
    grad_edges = grad_pre.astype(jnp.float32)
    bias_local = jnp.sum(grad_edges, axis=0)
    grad_mesh_proj = jax.ops.segment_sum(grad_edges, safe_node, num_segments=mesh_count).astype(
        jnp.bfloat16
    )
    returned = lax.all_to_all(
        grad_pre.reshape(patches, capacity, slice_width),
        "patch",
        split_axis=0,
        concat_axis=0,
        tiled=True,
    )
    per_edge = returned.reshape(slots, slice_width)[slot_index]
    grad_projected = jax.ops.segment_sum(
        per_edge.astype(jnp.float32), edge_source, num_segments=grid_count
    ).astype(jnp.bfloat16)
    dest_local = contract_rows(mesh_full, grad_mesh_proj)
    source_local = contract_rows(grid_full, grad_projected)
    node_full = lax.all_gather(grad_mesh_proj, "chan", axis=1, tiled=True)
    grad_mesh = (
        cotan_full
        + contract_cols(node_full, lax.dynamic_slice_in_dim(w_dest, offset, slice_width, 0))
    ).astype(jnp.bfloat16)
    source_full = lax.all_gather(grad_projected, "chan", axis=1, tiled=True)
    grad_grid = contract_cols(
        source_full, lax.dynamic_slice_in_dim(w_source, offset, slice_width, 0)
    ).astype(jnp.bfloat16)
    grad_w_source, grad_w_dest, grad_w_out, grad_bias, grad_gain = lax.psum(
        (source_local, dest_local, out_local, bias_local, gain_local), "patch"
    )
    return (
        updated,
        grad_grid,
        grad_mesh,
        grad_w_source,
        grad_w_dest,
        grad_w_out,
        grad_bias,
        grad_gain,
    )


MESH = pl.DeviceIdType.MESH
f32, bf16 = jnp.float32, jnp.bfloat16


def fused_kernel(
    P_, C_, B_,
    grid_hbm, mesh_hbm, cot_hbm, bias_hbm, gain_hbm, src_hbm, patch_hbm, node_hbm,
    ws_hbm, wd_hbm, wo_hbm,
    upd_ref, ggrid_ref, gmesh_ref, gws_ref, gwd_ref, gwo_ref, gbias_ref, ggain_ref,
    ws_col, ws_row, wd_col, wd_row, wo,
    gridz, meshb, cotb, gainb, bias_ref, gain_ref, ends,
    mp, ps, pr, qs, qr, qn, sm, nrm, gm, gs, gmn, gp, gmp, ns, nt,
    ends_h, src_t, dst_t, slope, grid_t, gpz, wsend, wrecv, bsend, brecv,
    w_sem, c_send, c_recv, p_send, p_recv, z_send, z_recv, s_send, s_recv, x_send, x_recv,
):
    me_p, me_c = lax.axis_index("patch"), lax.axis_index("chan")
    G, W = grid_hbm.shape
    M = mesh_hbm.shape[0]
    L = C_ * W
    E = src_hbm.shape[1]
    N = P_ * M
    H_ = P_ // B_
    lo, hi = lax.rem(me_p, B_), me_p // B_
    started = []

    def within(x, n):
        return jnp.where(x >= n, x - n, x)

    aheads = [within(hi + k % H_, H_) * B_ + within(lo + k // H_, B_) for k in range(P_)]
    behinds = [within(hi + (H_ - k % H_) % H_, H_) * B_ + within(lo + (B_ - k // H_) % B_, B_) for k in range(P_)]
    chans = [within(me_c + j, C_) for j in range(C_)]

    barrier = pltpu.get_barrier_semaphore()
    for k in range(1, P_):
        pl.semaphore_signal(barrier, inc=1, device_id=(aheads[k], me_c), device_id_type=MESH)
    for j in range(1, C_):
        pl.semaphore_signal(barrier, inc=1, device_id=(me_p, chans[j]), device_id_type=MESH)

    cols = pl.ds(pl.multiple_of(me_c * W, W), W)
    fills = [
        pltpu.make_async_copy(src, dst, w_sem.at[5 + i]) for i, (src, dst) in enumerate((
            (mesh_hbm, meshb.at[me_c]), (grid_hbm, gridz.at[me_c, 0]), (cot_hbm, cotb.at[me_c]),
            (gain_hbm, gain_ref), (bias_hbm, bias_ref), (src_hbm, ends.at[0, :, pl.ds(0, E)]),
            (patch_hbm, ends.at[0, :, pl.ds(E, E)]), (node_hbm, ends.at[0, :, pl.ds(2 * E, E)])))]
    loads = [
        pltpu.make_async_copy(wd_hbm.at[:, cols], wd_col, w_sem.at[0]),
        pltpu.make_async_copy(ws_hbm.at[:, cols], ws_col, w_sem.at[1]),
        pltpu.make_async_copy(wo_hbm, wo, w_sem.at[2]),
        pltpu.make_async_copy(wd_hbm.at[cols, :], wd_row, w_sem.at[3]),
        pltpu.make_async_copy(ws_hbm.at[cols, :], ws_row, w_sem.at[4]),
    ]
    for load in fills + loads:
        load.start()

    def remote(src, dst, send_sem, recv_sem, to):
        copy = pltpu.make_async_remote_copy(
            src_ref=src, dst_ref=dst, send_sem=send_sem, recv_sem=recv_sem,
            device_id=to, device_id_type=MESH)
        copy.start()
        started.append(copy)
        return copy

    def chan_gather(phase, src, buf):
        return [
            remote(src, buf.at[me_c], c_send.at[phase, j], c_recv.at[phase, j],
                   (me_p, chans[j]))
            for j in range(1, C_)]

    def patch_gather(phase, src, slot):
        return [
            remote(src, slot(k), p_send.at[phase, k], p_recv.at[phase, k], (aheads[k], me_c))
            for k in range(1, P_)]

    def patch_scatter(phase, block, buf):
        return [
            remote(block(k), buf.at[k], p_send.at[phase, k], p_recv.at[phase, k], (behinds[k], me_c))
            for k in range(1, P_)]

    def line_gather(phase, slot):
        return [
            remote(slot(0), slot(h), z_send.at[phase, h], z_recv.at[phase, h], (aheads[h], me_c))
            for h in range(1, H_)]

    def beside(phase, view):
        return [
            remote(view(0), view(b), x_send.at[phase, b], x_recv.at[phase, b], (aheads[b * H_], me_c))
            for b in range(1, B_)]

    even = C_ % 2 == 0
    twin = me_c + 1 - 2 * lax.rem(me_c, 2)

    def spread(phase, view):
        if not even:
            return [], [
                remote(view(me_c), view(me_c), s_send.at[phase, j], s_recv.at[phase, j],
                       (me_p, chans[j]))
                for j in range(1, C_)]
        near = [remote(view(me_c), view(me_c), s_send.at[phase, 0], s_recv.at[phase, 0], (me_p, twin))]
        across = [
            remote(view(me_c), view(me_c), s_send.at[phase, j], s_recv.at[phase, j],
                   (me_p, chans[2 * j]))
            for j in range(1, C_ // 2)]
        return near, across

    def spread_on(phase, view, across):
        arrived(across)
        if not even:
            return []
        passed = []
        for j in range(1, C_ // 2):
            block = view(chans[C_ - 2 * j])
            passed.append(remote(
                block, block, s_send.at[phase, C_ // 2 + j], s_recv.at[phase, C_ // 2 + j], (me_p, twin)))
        return passed

    def arrived(copies):
        for copy in copies:
            copy.wait_recv()

    def wide(buf):
        return jnp.concatenate([buf[c] for c in range(C_)], axis=1)

    def dot(a, b):
        return lax.dot_general(a, b, (((1,), (0,)), ((), ())), preferred_element_type=f32)

    def onehot_of(mask):
        return jnp.where(mask, 1.0, 0.0).astype(bf16)

    def flat(buf):
        return buf[...].reshape(N, W)

    def band_ends(h):
        row = ends[h]
        patch = row[:, E:2 * E]
        line = jnp.zeros_like(patch)
        for z in range(1, H_):
            line = line + jnp.where(patch >= z * B_, 1, 0)
        side = lo - (patch - line * B_)
        side = jnp.where(side < 0, side + B_, side)
        line = hi - line
        line = jnp.where(line < 0, line + H_, line)
        return row[:, :E], (side * H_ + line) * M + row[:, 2 * E:]

    def band_onehots(h):
        src, dst = band_ends(h)
        down = jnp.transpose(jnp.broadcast_to(jnp.concatenate([src, dst], axis=1), (128, 2 * E)))
        lane = lax.broadcasted_iota(jnp.int32, (E, 128), 1)
        for b in range(0, G, 128):
            ends_h[h, :, b:b + 128] = onehot_of(down[:E] == lane + b)
        for b in range(0, N, 128):
            ends_h[h, :, G + b:G + b + 128] = onehot_of(down[E:] == lane + b)
        src_t[h] = onehot_of(lax.broadcasted_iota(jnp.int32, (G, E), 0) == src)

    def band_full(h):
        return jnp.concatenate([gridz[c, h] for c in range(C_)], axis=1)

    def sigmoid(pre):
        return 1.0 / (1.0 + jnp.exp(-pre))

    def silu_slope(pre, sig):
        return sig * (1.0 + pre * (1.0 - sig))

    fills[0].wait()
    pl.semaphore_wait(barrier, P_ + C_ - 2)
    mesh_in = chan_gather(0, meshb.at[me_c], meshb)
    for fill in fills[1:]:
        fill.wait()
    grid_in = chan_gather(1, gridz.at[me_c, 0], gridz.at[:, 0])
    ends_in = line_gather(1, lambda h: ends.at[h])
    gainb[me_c] = jnp.broadcast_to(gain_ref[...], gainb.shape[1:])
    ns[0, me_c, 0] = meshb[me_c]
    nodes_line = line_gather(2, lambda h: ns.at[0, me_c, h])
    line_in = line_gather(0, lambda h: gridz.at[me_c, h, pl.ds(0, G // 4)])

    loads[0].wait()
    arrived(mesh_in)
    mp[0] = (dot(wide(meshb), wd_col[...]) + bias_ref[...]).astype(bf16)
    mp_in = patch_gather(0, mp.at[0], lambda k: mp.at[k])
    line_in += line_gather(3, lambda h: gridz.at[me_c, h, pl.ds(G // 4, 3 * G // 4)])
    cot_in = chan_gather(2, cotb.at[me_c], cotb)
    gain_in = chan_gather(3, gainb.at[me_c], gainb)

    band_onehots(0)
    dst_t[...] = onehot_of(lax.broadcasted_iota(jnp.int32, (N, E), 0) == band_ends(0)[1])
    loads[1].wait()
    arrived(grid_in)
    projected = dot(band_full(0), ws_col[...]).astype(bf16)
    sender = dot(ends_h[0, :, :G], projected)
    arrived(nodes_line)
    nodes_in = beside(2, lambda b: ns.at[0, me_c, pl.ds(b * H_, H_)])

    arrived(mp_in)
    pre = sender + dot(ends_h[0, :, G:], flat(mp))
    sig = sigmoid(pre)
    part = dot(dst_t[...], (pre * sig).astype(bf16))
    ps[...] = part.astype(bf16).reshape(P_, M, W)
    part_in = patch_scatter(1, lambda k: ps.at[k], pr)
    own_slope = silu_slope(pre, sig)
    slope[0] = own_slope
    turned = dot(dst_t[...], own_slope.astype(bf16))
    qs[...] = turned.astype(bf16).reshape(P_, M, W)
    turned_in = patch_scatter(2, lambda k: qs.at[k], qr)
    total = part[:M]
    slope_total = turned[:M]

    arrived(ends_in)

    def other_onehots(h, carry):
        band_onehots(h)
        return carry

    lax.fori_loop(1, H_, other_onehots, 0)
    grid_t[:, 0:G] = jnp.transpose(band_full(0))
    arrived(line_in)
    bands = lambda c: gridz.at[c, pl.ds(1, H_ - 1)]
    band_near, band_across = spread(0, bands)

    arrived(part_in)
    for k in range(1, P_):
        total = total + pr[k].astype(f32)
    sm[me_c] = total.astype(bf16)
    sm_in = chan_gather(4, sm.at[me_c], sm)
    ns[1, me_c, 0] = total.astype(bf16)
    sums_in = patch_gather(4, sm.at[me_c], lambda k: ns.at[1, me_c, k])
    arrived(nodes_in)
    nodes = lambda c: ns.at[0, c]
    nodes_near, nodes_across = spread(1, nodes)
    arrived(turned_in)
    for k in range(1, P_):
        slope_total = slope_total + qr[k].astype(f32)
    qn[0] = slope_total.astype(bf16)
    qn_line = line_gather(4, lambda h: qn.at[h])

    loads[2].wait()
    arrived(cot_in)
    arrived(gain_in)
    gain_full = jnp.concatenate([gainb[c][0:1] for c in range(C_)], axis=1)
    scaled = wide(cotb).astype(f32) * gain_full
    scaled_mean = jnp.sum(scaled, axis=1, keepdims=True) / L
    arrived(sm_in)
    mixed = dot(wide(sm), wo[...])
    mean = jnp.sum(mixed, axis=1, keepdims=True) / L
    centred = mixed - mean
    var = jnp.sum(centred * centred, axis=1, keepdims=True) / L
    inv = lax.rsqrt(var + norm_eps)
    normed = centred * inv
    cross_mean = jnp.sum(scaled * normed, axis=1, keepdims=True) / L
    grad_mixed = ((scaled - scaled_mean - normed * cross_mean) * inv).astype(bf16)
    grad_summed = contract_cols(grad_mixed, wo[cols, :])
    gs[0] = grad_summed.astype(bf16)
    gs_in = patch_gather(6, gs.at[0], lambda k: gs.at[k])

    grad_nodes = grad_summed * slope_total
    gmp[me_c] = grad_nodes.astype(bf16)
    gmp_in = chan_gather(6, gmp.at[me_c], gmp)
    band_passed = spread_on(0, bands, band_across)
    for c in range(C_):
        nrm[c] = normed[:, c * W:(c + 1) * W]
        gm[c] = grad_mixed[:, c * W:(c + 1) * W]
    gmn[0] = gm[me_c]
    own_normed = nrm[me_c]
    cot_own = cotb[me_c].astype(f32)
    bsend[...] = jnp.concatenate(
        [jnp.sum(grad_nodes, axis=0, keepdims=True),
         jnp.sum(cot_own * own_normed, axis=0, keepdims=True), jnp.zeros((6, W), f32)], axis=0)
    small_in = patch_gather(8, bsend, lambda k: brecv.at[k])
    upd_ref[...] = (meshb[me_c].astype(f32) + own_normed * gain_ref[...]).astype(bf16)

    gmn_in = patch_gather(7, gmn.at[0], lambda k: gmn.at[k])
    arrived(sums_in)
    sums = lambda c: ns.at[1, c]
    sums_near, sums_across = spread(2, sums)

    arrived(band_near)
    arrived(band_passed)

    def other_slopes(h, carry):
        full = band_full(h)
        grid_t[:, pl.ds(pl.multiple_of(h * G, G), G)] = jnp.transpose(full)
        pre = dot(ends_h[h, :, :G], dot(full, ws_col[...]).astype(bf16)) + dot(ends_h[h, :, G:], flat(mp))
        slope[h] = silu_slope(pre, sigmoid(pre))
        return carry

    lax.fori_loop(1, H_, other_slopes, 0)
    arrived(qn_line)
    qn_in = beside(3, lambda b: qn.at[pl.ds(b * H_, H_)])
    nodes_passed = spread_on(1, nodes, nodes_across)
    loads[3].wait()
    loads[4].wait()
    arrived(gmp_in)
    gmesh_ref[...] = (cot_own + contract_cols(wide(gmp), wd_row[...])).astype(bf16)

    def turn(i, c):
        nt[c, i] = jnp.transpose(ns[i, c].reshape(N, W))

    turn(1, me_c)
    arrived(nodes_near)
    arrived(nodes_passed)
    for c in range(C_):
        turn(0, c)
    if even:
        arrived(sums_near)
        turn(1, twin)

    def band_grad(h):
        grad_pre = (dot(ends_h[h, :, G:], flat(gs)) * slope[h]).astype(bf16)
        return dot(src_t[h], grad_pre).astype(bf16)

    arrived(gs_in)
    grad_projected = band_grad(0)
    gp[me_c] = grad_projected
    gp_in = chan_gather(5, gp.at[me_c], gp)
    gpz[0:G] = grad_projected
    for h in range(1, H_):
        gpz[h * G:(h + 1) * G] = band_grad(h)
    weight_in = []
    half = L // 2
    for i in range(2):
        piece = pl.ds(i * half, half)
        wsend[piece] = dot(grid_t[piece, :], gpz[...]).astype(bf16)
        weight_in += [
            remote(wsend.at[piece], wrecv.at[b, piece], x_send.at[i, b], x_recv.at[i, b],
                   (aheads[b * H_], me_c))
            for b in range(1, B_)]

    sums_passed = spread_on(2, sums, sums_across)
    arrived(sums_passed)
    for j in range(1, C_ // 2 if even else C_):
        turn(1, chans[C_ - (2 * j if even else j)])
    if even:
        for j in range(1, C_ // 2):
            turn(1, lax.rem(twin + C_ - 2 * j, C_))
    arrived(qn_in)
    grad_nodes_all = (flat(gs).astype(f32) * flat(qn).astype(f32)).astype(bf16)
    for c in range(C_):
        gwd_ref[c * W:(c + 1) * W, :] = dot(nt[c, 0], grad_nodes_all)
    arrived(gmn_in)
    for c in range(C_):
        gwo_ref[c * W:(c + 1) * W, :] = dot(nt[c, 1], flat(gmn))
    arrived(small_in)
    small = bsend[...]
    for k in range(1, P_):
        small = small + brecv[k]
    gbias_ref[...] = small[0:1]
    ggain_ref[...] = small[1:2]
    arrived(gp_in)
    ggrid_ref[...] = contract_cols(wide(gp), ws_row[...]).astype(bf16)
    arrived(weight_in)
    source = wsend[...].astype(f32)
    for b in range(1, B_):
        source = source + wrecv[b].astype(f32)
    gws_ref[...] = source
    for copy in started:
        copy.wait_send()


def write_out(*refs):
    sems = refs[-1]
    copies = [
        pltpu.make_async_copy(refs[i], refs[8 + i], sems.at[i]) for i in range(8)]
    for copy in copies:
        copy.start()
    for copy in copies:
        copy.wait()


def fused_on_device(
    patches, chans,
    grid_latent, mesh_latent, w_source, w_dest, w_out, edge_bias, norm_gain,
    edge_source, edge_patch, edge_node, cotangent,
):
    G, W = grid_latent.shape
    M = mesh_latent.shape[0]
    L = w_source.shape[0]
    E = edge_source.shape[0]
    N = patches * M
    near = 2 if patches % 2 == 0 else 1
    far = patches // near
    vmem = pl.BlockSpec(memory_space=pltpu.VMEM)
    hbm = pl.BlockSpec(memory_space=pltpu.HBM)
    sds = jax.ShapeDtypeStruct

    def buf(*shape, dtype=bf16):
        return pltpu.VMEM(shape, dtype)

    def sems(*shape):
        return [pltpu.SemaphoreType.DMA(shape), pltpu.SemaphoreType.DMA(shape)]

    nodes = buf(patches, M, W)
    outs = pl.pallas_call(
        functools.partial(fused_kernel, patches, chans, near),
        out_shape=(
            sds((M, W), bf16), sds((G, W), bf16), sds((M, W), bf16),
            sds((L, W), f32), sds((L, W), f32), sds((L, W), f32),
            sds((1, W), f32), sds((1, W), f32),
        ),
        in_specs=[hbm] * 11,
        out_specs=(vmem,) * 8,
        scratch_shapes=[
            buf(L, W), buf(W, L), buf(L, W), buf(W, L), buf(L, L),
            buf(chans, far, G, W), buf(chans, M, W), buf(chans, M, W), buf(chans, 8, W, dtype=f32),
            buf(1, W, dtype=f32), buf(1, W, dtype=f32), buf(far, 1, 3 * E, dtype=jnp.int32),
            nodes, nodes, nodes, nodes, nodes, nodes, buf(chans, M, W), buf(chans, M, W, dtype=f32),
            buf(chans, M, W), nodes, nodes, buf(chans, G, W), buf(chans, M, W),
            buf(2, chans, patches, M, W), buf(chans, 2, W, N),
            buf(far, E, G + N), buf(far, G, E), buf(N, E), buf(far, E, W, dtype=f32),
            buf(L, far * G), buf(far * G, W), buf(L, W), buf(near, L, W),
            buf(8, W, dtype=f32), buf(patches, 8, W, dtype=f32),
            pltpu.SemaphoreType.DMA((13,)),
            *sems(7, chans), *sems(9, patches), *sems(6, far), *sems(3, chans + 1), *sems(5, near),
        ],
        compiler_params=pltpu.CompilerParams(
            collective_id=0, has_side_effects=True, vmem_limit_bytes=60 * 1024 * 1024),
    )(
        grid_latent, mesh_latent, cotangent, edge_bias.reshape(1, W), norm_gain.reshape(1, W),
        edge_source.reshape(1, E), edge_patch.reshape(1, E), edge_node.reshape(1, E),
        w_source, w_dest, w_out,
    )
    outs = pl.pallas_call(
        write_out,
        out_shape=tuple(sds(out.shape, out.dtype) for out in outs),
        in_specs=[vmem] * 8,
        out_specs=(hbm,) * 8,
        scratch_shapes=[pltpu.SemaphoreType.DMA((8,))],
    )(*outs)
    return outs[:6] + (outs[6].reshape(W), outs[7].reshape(W))


def device_program(mesh):
    patches, chans = mesh.shape["patch"], mesh.shape["chan"]
    if patches <= 16:
        return functools.partial(fused_on_device, patches, chans)
    return on_device


def solution(mesh):
    placed = (
        P("patch", "chan"),
        P("patch", "chan"),
        P(),
        P(),
        P(),
        P("chan"),
        P("chan"),
        P("patch"),
        P("patch", None),
        P("patch"),
        P("patch", "chan"),
    )
    return jax.shard_map(
        device_program(mesh),
        mesh=mesh,
        in_specs=placed,
        out_specs=(
            P("patch", "chan"),
            P("patch", "chan"),
            P("patch", "chan"),
            P(None, "chan"),
            P(None, "chan"),
            P(None, "chan"),
            P("chan"),
            P("chan"),
        ),
        check_vma=False,
    )
```

```python
import functools
import math

import jax
import jax.numpy as jnp
from jax import lax
from jax.experimental import pallas as pl
from jax.experimental.pallas import tpu as pltpu
from jax.sharding import PartitionSpec as P

norm_eps = 1e-05


def slot_ranks(dest_patch, patches):
    edge_count = dest_patch.shape[0]
    block_width = math.gcd(edge_count, 128)
    onehot = (
        dest_patch.reshape(edge_count // block_width, block_width)[:, :, None]
        == jnp.arange(patches, dtype=jnp.int32)[None, None, :]
    ).astype(jnp.float32)
    strict_lower = (jnp.arange(block_width)[:, None] > jnp.arange(block_width)[None, :]).astype(
        jnp.float32
    )
    within = jnp.einsum("ij,bjp->bip", strict_lower, onehot, precision=lax.Precision.HIGHEST)
    counts = jnp.sum(onehot, axis=1)
    blocks = jnp.arange(counts.shape[0])
    earlier = (blocks[:, None] > blocks[None, :]).astype(jnp.float32)
    before = jnp.dot(earlier, counts, precision=lax.Precision.HIGHEST)
    position = jnp.sum((within + before[:, None, :]) * onehot, axis=2)
    return position.reshape(edge_count).astype(jnp.int32)


def contract_rows(left, right):
    return lax.dot_general(
        left, right, (((0,), (0,)), ((), ())), preferred_element_type=jnp.float32
    )


def contract_cols(left, right):
    return lax.dot_general(
        left, right, (((1,), (1,)), ((), ())), preferred_element_type=jnp.float32
    )


def on_device(
    grid_latent,
    mesh_latent,
    w_source,
    w_dest,
    w_out,
    edge_bias,
    norm_gain,
    edge_source,
    edge_patch,
    edge_node,
    cotangent,
):
    patches = lax.axis_size("patch")
    slice_width = grid_latent.shape[1]
    latent_width = w_source.shape[0]
    offset = lax.axis_index("chan") * slice_width
    grid_count = grid_latent.shape[0]
    mesh_count = mesh_latent.shape[0]
    edge_count = edge_source.shape[0]
    capacity = max(2, 2 * edge_count // patches)
    slots = patches * capacity
    dest_patch = edge_patch[:, 0]
    slot_index = dest_patch * capacity + slot_ranks(dest_patch, patches)
    grid_full = lax.all_gather(grid_latent, "chan", axis=1, tiled=True)
    mesh_full = lax.all_gather(mesh_latent, "chan", axis=1, tiled=True)
    source_cols = lax.dynamic_slice_in_dim(w_source, offset, slice_width, 1)
    dest_cols = lax.dynamic_slice_in_dim(w_dest, offset, slice_width, 1)
    out_cols = lax.dynamic_slice_in_dim(w_out, offset, slice_width, 1)
    mesh_proj = jnp.dot(mesh_full, dest_cols, preferred_element_type=jnp.float32)
    empty_rows = jnp.zeros((slots, slice_width), jnp.bfloat16)
    projected = jnp.dot(grid_full, source_cols, preferred_element_type=jnp.float32).astype(
        jnp.bfloat16
    )
    outgoing = empty_rows.at[slot_index].set(projected[edge_source])
    targets = jnp.full((slots,), mesh_count, jnp.int32).at[slot_index].set(edge_node)
    arrived = lax.all_to_all(
        outgoing.reshape(patches, capacity, slice_width),
        "patch",
        split_axis=0,
        concat_axis=0,
        tiled=True,
    )
    landed = lax.all_to_all(
        targets.reshape(patches, capacity), "patch", split_axis=0, concat_axis=0, tiled=True
    )
    edge_values = arrived.reshape(slots, slice_width)
    landed = landed.reshape(slots)
    is_live = landed < mesh_count
    safe_node = jnp.minimum(landed, mesh_count - 1)
    pre_act = edge_values.astype(jnp.float32) + mesh_proj[safe_node] + edge_bias
    message = jnp.where(is_live[:, None], jax.nn.silu(pre_act), 0.0)
    summed = jax.ops.segment_sum(message, safe_node, num_segments=mesh_count).astype(jnp.bfloat16)
    summed_full = lax.all_gather(summed, "chan", axis=1, tiled=True)
    mixed = jnp.dot(summed_full, out_cols, preferred_element_type=jnp.float32)
    row_total, row_square = lax.psum(
        (jnp.sum(mixed, axis=1), jnp.sum(mixed * mixed, axis=1)), "chan"
    )
    row_mean = row_total / latent_width
    row_var = jnp.maximum(row_square / latent_width - row_mean * row_mean, 0.0)
    inv_scale = lax.rsqrt(row_var + norm_eps)
    normed = (mixed - row_mean[:, None]) * inv_scale[:, None]
    updated = (mesh_latent.astype(jnp.float32) + normed * norm_gain).astype(jnp.bfloat16)
    cotan_full = cotangent.astype(jnp.float32)
    gain_local = jnp.sum(cotan_full * normed, axis=0)
    scaled = cotan_full * norm_gain
    scaled_total, cross_total = lax.psum(
        (jnp.sum(scaled, axis=1), jnp.sum(scaled * normed, axis=1)), "chan"
    )
    grad_mixed = (
        (
            scaled
            - scaled_total[:, None] / latent_width
            - normed * (cross_total[:, None] / latent_width)
        )
        * inv_scale[:, None]
    ).astype(jnp.bfloat16)
    out_local = contract_rows(summed_full, grad_mixed)
    grad_full = lax.all_gather(grad_mixed, "chan", axis=1, tiled=True)
    grad_summed = contract_cols(grad_full, lax.dynamic_slice_in_dim(w_out, offset, slice_width, 0))
    sigmoid_val = jax.nn.sigmoid(pre_act)
    silu_slope = sigmoid_val * (1.0 + pre_act * (1.0 - sigmoid_val))
    grad_pre = jnp.where(is_live[:, None], grad_summed[safe_node] * silu_slope, 0.0).astype(
        jnp.bfloat16
    )
    grad_edges = grad_pre.astype(jnp.float32)
    bias_local = jnp.sum(grad_edges, axis=0)
    grad_mesh_proj = jax.ops.segment_sum(grad_edges, safe_node, num_segments=mesh_count).astype(
        jnp.bfloat16
    )
    returned = lax.all_to_all(
        grad_pre.reshape(patches, capacity, slice_width),
        "patch",
        split_axis=0,
        concat_axis=0,
        tiled=True,
    )
    per_edge = returned.reshape(slots, slice_width)[slot_index]
    grad_projected = jax.ops.segment_sum(
        per_edge.astype(jnp.float32), edge_source, num_segments=grid_count
    ).astype(jnp.bfloat16)
    dest_local = contract_rows(mesh_full, grad_mesh_proj)
    source_local = contract_rows(grid_full, grad_projected)
    node_full = lax.all_gather(grad_mesh_proj, "chan", axis=1, tiled=True)
    grad_mesh = (
        cotan_full
        + contract_cols(node_full, lax.dynamic_slice_in_dim(w_dest, offset, slice_width, 0))
    ).astype(jnp.bfloat16)
    source_full = lax.all_gather(grad_projected, "chan", axis=1, tiled=True)
    grad_grid = contract_cols(
        source_full, lax.dynamic_slice_in_dim(w_source, offset, slice_width, 0)
    ).astype(jnp.bfloat16)
    grad_w_source, grad_w_dest, grad_w_out, grad_bias, grad_gain = lax.psum(
        (source_local, dest_local, out_local, bias_local, gain_local), "patch"
    )
    return (
        updated,
        grad_grid,
        grad_mesh,
        grad_w_source,
        grad_w_dest,
        grad_w_out,
        grad_bias,
        grad_gain,
    )


MESH = pl.DeviceIdType.MESH
f32, bf16 = jnp.float32, jnp.bfloat16


def fused_kernel(
    P_, C_, B_,
    grid_hbm, mesh_hbm, cot_hbm, bias_hbm, gain_hbm, src_hbm, patch_hbm, node_hbm,
    ws_hbm, wd_hbm, wo_hbm,
    upd_ref, ggrid_ref, gmesh_ref, gws_ref, gwd_ref, gwo_ref, gbias_ref, ggain_ref,
    ws_col, ws_row, wd_col, wd_row, wo,
    gridz, meshb, cotb, gainb, bias_ref, gain_ref, ends,
    mp, ps, pr, qs, qr, qn, sm, nrm, gm, gs, gmn, gp, gmp, ns, nt,
    ends_h, src_t, dst_t, slope, grid_t, gpz, wsend, wrecv, bsend, brecv,
    w_sem, c_send, c_recv, p_send, p_recv, z_send, z_recv, s_send, s_recv, x_send, x_recv,
):
    me_p, me_c = lax.axis_index("patch"), lax.axis_index("chan")
    G, W = grid_hbm.shape
    M = mesh_hbm.shape[0]
    L = C_ * W
    E = src_hbm.shape[1]
    N = P_ * M
    H_ = P_ // B_
    lo, hi = lax.rem(me_p, B_), me_p // B_
    started = []

    def within(x, n):
        return jnp.where(x >= n, x - n, x)

    aheads = [within(hi + k % H_, H_) * B_ + within(lo + k // H_, B_) for k in range(P_)]
    behinds = [within(hi + (H_ - k % H_) % H_, H_) * B_ + within(lo + (B_ - k // H_) % B_, B_) for k in range(P_)]
    chans = [within(me_c + j, C_) for j in range(C_)]

    barrier = pltpu.get_barrier_semaphore()
    for k in range(1, P_):
        pl.semaphore_signal(barrier, inc=1, device_id=(aheads[k], me_c), device_id_type=MESH)
    for j in range(1, C_):
        pl.semaphore_signal(barrier, inc=1, device_id=(me_p, chans[j]), device_id_type=MESH)

    cols = pl.ds(pl.multiple_of(me_c * W, W), W)
    fills = [
        pltpu.make_async_copy(src, dst, w_sem.at[5 + i]) for i, (src, dst) in enumerate((
            (mesh_hbm, meshb.at[me_c]), (grid_hbm, gridz.at[me_c, 0]), (cot_hbm, cotb.at[me_c]),
            (gain_hbm, gain_ref), (bias_hbm, bias_ref), (src_hbm, ends.at[0, :, pl.ds(0, E)]),
            (patch_hbm, ends.at[0, :, pl.ds(E, E)]), (node_hbm, ends.at[0, :, pl.ds(2 * E, E)])))]
    loads = [
        pltpu.make_async_copy(wd_hbm.at[:, cols], wd_col, w_sem.at[0]),
        pltpu.make_async_copy(ws_hbm.at[:, cols], ws_col, w_sem.at[1]),
        pltpu.make_async_copy(wo_hbm, wo, w_sem.at[2]),
        pltpu.make_async_copy(wd_hbm.at[cols, :], wd_row, w_sem.at[3]),
        pltpu.make_async_copy(ws_hbm.at[cols, :], ws_row, w_sem.at[4]),
    ]
    for load in fills + loads:
        load.start()

    def remote(src, dst, send_sem, recv_sem, to):
        copy = pltpu.make_async_remote_copy(
            src_ref=src, dst_ref=dst, send_sem=send_sem, recv_sem=recv_sem,
            device_id=to, device_id_type=MESH)
        copy.start()
        started.append(copy)
        return copy

    def chan_gather(phase, src, buf):
        return [
            remote(src, buf.at[me_c], c_send.at[phase, j], c_recv.at[phase, j],
                   (me_p, chans[j]))
            for j in range(1, C_)]

    def patch_gather(phase, src, slot):
        return [
            remote(src, slot(k), p_send.at[phase, k], p_recv.at[phase, k], (aheads[k], me_c))
            for k in range(1, P_)]

    def patch_scatter(phase, block, buf):
        return [
            remote(block(k), buf.at[k], p_send.at[phase, k], p_recv.at[phase, k], (behinds[k], me_c))
            for k in range(1, P_)]

    def line_gather(phase, slot):
        return [
            remote(slot(0), slot(h), z_send.at[phase, h], z_recv.at[phase, h], (aheads[h], me_c))
            for h in range(1, H_)]

    def beside(phase, view):
        return [
            remote(view(0), view(b), x_send.at[phase, b], x_recv.at[phase, b], (aheads[b * H_], me_c))
            for b in range(1, B_)]

    even = C_ % 2 == 0
    twin = me_c + 1 - 2 * lax.rem(me_c, 2)

    def spread(phase, view):
        if not even:
            return [], [
                remote(view(me_c), view(me_c), s_send.at[phase, j], s_recv.at[phase, j],
                       (me_p, chans[j]))
                for j in range(1, C_)]
        near = [remote(view(me_c), view(me_c), s_send.at[phase, 0], s_recv.at[phase, 0], (me_p, twin))]
        across = [
            remote(view(me_c), view(me_c), s_send.at[phase, j], s_recv.at[phase, j],
                   (me_p, chans[2 * j]))
            for j in range(1, C_ // 2)]
        return near, across

    def spread_on(phase, view, across):
        arrived(across)
        if not even:
            return []
        passed = []
        for j in range(1, C_ // 2):
            block = view(chans[C_ - 2 * j])
            passed.append(remote(
                block, block, s_send.at[phase, C_ // 2 + j], s_recv.at[phase, C_ // 2 + j], (me_p, twin)))
        return passed

    def arrived(copies):
        for copy in copies:
            copy.wait_recv()

    def wide(buf):
        return jnp.concatenate([buf[c] for c in range(C_)], axis=1)

    def dot(a, b):
        return lax.dot_general(a, b, (((1,), (0,)), ((), ())), preferred_element_type=f32)

    def onehot_of(mask):
        return jnp.where(mask, 1.0, 0.0).astype(bf16)

    def flat(buf):
        return buf[...].reshape(N, W)

    def band_ends(h):
        row = ends[h]
        patch = row[:, E:2 * E]
        line = jnp.zeros_like(patch)
        for z in range(1, H_):
            line = line + jnp.where(patch >= z * B_, 1, 0)
        side = lo - (patch - line * B_)
        side = jnp.where(side < 0, side + B_, side)
        line = hi - line
        line = jnp.where(line < 0, line + H_, line)
        return row[:, :E], (side * H_ + line) * M + row[:, 2 * E:]

    def band_onehots(h):
        src, dst = band_ends(h)
        down = jnp.transpose(jnp.broadcast_to(jnp.concatenate([src, dst], axis=1), (128, 2 * E)))
        lane = lax.broadcasted_iota(jnp.int32, (E, 128), 1)
        for b in range(0, G, 128):
            ends_h[h, :, b:b + 128] = onehot_of(down[:E] == lane + b)
        for b in range(0, N, 128):
            ends_h[h, :, G + b:G + b + 128] = onehot_of(down[E:] == lane + b)
        src_t[h] = onehot_of(lax.broadcasted_iota(jnp.int32, (G, E), 0) == src)

    def band_full(h):
        return jnp.concatenate([gridz[c, h] for c in range(C_)], axis=1)

    def sigmoid(pre):
        return 1.0 / (1.0 + jnp.exp(-pre))

    def silu_slope(pre, sig):
        return sig * (1.0 + pre * (1.0 - sig))

    fills[0].wait()
    pl.semaphore_wait(barrier, P_ + C_ - 2)
    mesh_in = chan_gather(0, meshb.at[me_c], meshb)
    for fill in fills[1:]:
        fill.wait()
    grid_in = chan_gather(1, gridz.at[me_c, 0], gridz.at[:, 0])
    ends_in = line_gather(1, lambda h: ends.at[h])
    gainb[me_c] = jnp.broadcast_to(gain_ref[...], gainb.shape[1:])
    ns[0, me_c, 0] = meshb[me_c]
    nodes_line = line_gather(2, lambda h: ns.at[0, me_c, h])
    line_in = line_gather(0, lambda h: gridz.at[me_c, h, pl.ds(0, 3 * G // 8)])

    loads[0].wait()
    arrived(mesh_in)
    mp[0] = (dot(wide(meshb), wd_col[...]) + bias_ref[...]).astype(bf16)
    mp_in = patch_gather(0, mp.at[0], lambda k: mp.at[k])
    line_in += line_gather(3, lambda h: gridz.at[me_c, h, pl.ds(3 * G // 8, 5 * G // 8)])
    cot_in = chan_gather(2, cotb.at[me_c], cotb)
    gain_in = chan_gather(3, gainb.at[me_c], gainb)

    band_onehots(0)
    dst_t[...] = onehot_of(lax.broadcasted_iota(jnp.int32, (N, E), 0) == band_ends(0)[1])
    loads[1].wait()
    arrived(grid_in)
    projected = dot(band_full(0), ws_col[...]).astype(bf16)
    sender = dot(ends_h[0, :, :G], projected)
    arrived(nodes_line)
    nodes_in = beside(2, lambda b: ns.at[0, me_c, pl.ds(b * H_, H_)])

    arrived(mp_in)
    pre = sender + dot(ends_h[0, :, G:], flat(mp))
    sig = sigmoid(pre)
    part = dot(dst_t[...], (pre * sig).astype(bf16))
    ps[...] = part.astype(bf16).reshape(P_, M, W)
    part_in = patch_scatter(1, lambda k: ps.at[k], pr)
    own_slope = silu_slope(pre, sig)
    slope[0] = own_slope
    turned = dot(dst_t[...], own_slope.astype(bf16))
    qs[...] = turned.astype(bf16).reshape(P_, M, W)
    turned_side = [
        remote(qs.at[pl.ds(b * H_, H_)], qr.at[pl.ds(b * H_, H_)], x_send.at[3, b], x_recv.at[3, b],
               (behinds[b * H_], me_c))
        for b in range(1, B_)]
    total = part[:M]
    line_slopes = turned[:H_ * M].reshape(H_, M, W)

    arrived(ends_in)

    def other_onehots(h, carry):
        band_onehots(h)
        return carry

    lax.fori_loop(1, H_, other_onehots, 0)
    grid_t[:, 0:G] = jnp.transpose(band_full(0))
    arrived(line_in)
    bands = lambda c: gridz.at[c, pl.ds(1, H_ - 1)]
    band_near, band_across = spread(0, bands)

    arrived(turned_side)
    for b in range(1, B_):
        line_slopes = line_slopes + qr[b * H_:(b + 1) * H_].astype(f32)
    qs[0:H_] = line_slopes.astype(bf16)
    turned_in = [
        remote(qs.at[h], qr.at[h], z_send.at[4, h], z_recv.at[4, h], (behinds[h], me_c))
        for h in range(1, H_)]
    arrived(part_in)
    for k in range(1, P_):
        total = total + pr[k].astype(f32)
    sm[me_c] = total.astype(bf16)
    sm_in = chan_gather(4, sm.at[me_c], sm)
    ns[1, me_c, 0] = total.astype(bf16)
    sums_in = patch_gather(4, sm.at[me_c], lambda k: ns.at[1, me_c, k])
    arrived(nodes_in)
    nodes = lambda c: ns.at[0, c]
    nodes_near, nodes_across = spread(1, nodes)
    loads[2].wait()
    arrived(cot_in)
    arrived(gain_in)
    gain_full = jnp.concatenate([gainb[c][0:1] for c in range(C_)], axis=1)
    scaled = wide(cotb).astype(f32) * gain_full
    scaled_mean = jnp.sum(scaled, axis=1, keepdims=True) / L
    arrived(sm_in)
    mixed = dot(wide(sm), wo[...])
    mean = jnp.sum(mixed, axis=1, keepdims=True) / L
    centred = mixed - mean
    var = jnp.sum(centred * centred, axis=1, keepdims=True) / L
    inv = lax.rsqrt(var + norm_eps)
    normed = centred * inv
    cross_mean = jnp.sum(scaled * normed, axis=1, keepdims=True) / L
    grad_mixed = ((scaled - scaled_mean - normed * cross_mean) * inv).astype(bf16)
    grad_summed = contract_cols(grad_mixed, wo[cols, :])
    gs[0] = grad_summed.astype(bf16)
    gs_in = patch_gather(6, gs.at[0], lambda k: gs.at[k])

    arrived(turned_in)
    slope_total = line_slopes[0]
    for h in range(1, H_):
        slope_total = slope_total + qr[h].astype(f32)
    grad_nodes = grad_summed * slope_total
    gmp[me_c] = grad_nodes.astype(bf16)
    gmp_in = chan_gather(6, gmp.at[me_c], gmp)
    band_passed = spread_on(0, bands, band_across)
    for c in range(C_):
        nrm[c] = normed[:, c * W:(c + 1) * W]
        gm[c] = grad_mixed[:, c * W:(c + 1) * W]
    gmn[0] = gm[me_c]
    own_normed = nrm[me_c]
    cot_own = cotb[me_c].astype(f32)
    bsend[...] = jnp.concatenate(
        [jnp.sum(grad_nodes, axis=0, keepdims=True),
         jnp.sum(cot_own * own_normed, axis=0, keepdims=True), jnp.zeros((6, W), f32)], axis=0)
    small_in = patch_gather(8, bsend, lambda k: brecv.at[k])
    upd_ref[...] = (meshb[me_c].astype(f32) + own_normed * gain_ref[...]).astype(bf16)

    gmn_in = patch_gather(7, gmn.at[0], lambda k: gmn.at[k])
    qn[0] = grad_nodes.astype(bf16)
    qn_in = patch_gather(5, qn.at[0], lambda k: qn.at[k])
    arrived(sums_in)
    sums = lambda c: ns.at[1, c]
    sums_near, sums_across = spread(2, sums)

    arrived(band_near)
    arrived(band_passed)

    def other_slopes(h, carry):
        full = band_full(h)
        grid_t[:, pl.ds(pl.multiple_of(h * G, G), G)] = jnp.transpose(full)
        pre = dot(ends_h[h, :, :G], dot(full, ws_col[...]).astype(bf16)) + dot(ends_h[h, :, G:], flat(mp))
        slope[h] = silu_slope(pre, sigmoid(pre))
        return carry

    lax.fori_loop(1, H_, other_slopes, 0)
    nodes_passed = spread_on(1, nodes, nodes_across)
    loads[3].wait()
    loads[4].wait()
    arrived(gmp_in)
    gmesh_ref[...] = (cot_own + contract_cols(wide(gmp), wd_row[...])).astype(bf16)

    def turn(i, c):
        nt[c, i] = jnp.transpose(ns[i, c].reshape(N, W))

    turn(1, me_c)
    arrived(nodes_near)
    arrived(nodes_passed)
    for c in range(C_):
        turn(0, c)
    if even:
        arrived(sums_near)
        turn(1, twin)

    def band_grad(h):
        grad_pre = (dot(ends_h[h, :, G:], flat(gs)) * slope[h]).astype(bf16)
        return dot(src_t[h], grad_pre).astype(bf16)

    arrived(gs_in)
    grad_projected = band_grad(0)
    gp[me_c] = grad_projected
    gp_in = chan_gather(5, gp.at[me_c], gp)
    gpz[0:G] = grad_projected
    for h in range(1, H_):
        gpz[h * G:(h + 1) * G] = band_grad(h)
    weight_in = []
    half = L // 2
    for i in range(2):
        piece = pl.ds(i * half, half)
        wsend[piece] = dot(grid_t[piece, :], gpz[...]).astype(bf16)
        weight_in += [
            remote(wsend.at[piece], wrecv.at[b, piece], x_send.at[i, b], x_recv.at[i, b],
                   (aheads[b * H_], me_c))
            for b in range(1, B_)]

    sums_passed = spread_on(2, sums, sums_across)
    arrived(sums_passed)
    for j in range(1, C_ // 2 if even else C_):
        turn(1, chans[C_ - (2 * j if even else j)])
    if even:
        for j in range(1, C_ // 2):
            turn(1, lax.rem(twin + C_ - 2 * j, C_))
    arrived(gmn_in)
    for c in range(C_):
        gwo_ref[c * W:(c + 1) * W, :] = dot(nt[c, 1], flat(gmn))
    arrived(qn_in)
    grad_nodes_all = flat(qn)
    for c in range(C_):
        gwd_ref[c * W:(c + 1) * W, :] = dot(nt[c, 0], grad_nodes_all)
    arrived(small_in)
    small = bsend[...]
    for k in range(1, P_):
        small = small + brecv[k]
    gbias_ref[...] = small[0:1]
    ggain_ref[...] = small[1:2]
    arrived(gp_in)
    ggrid_ref[...] = contract_cols(wide(gp), ws_row[...]).astype(bf16)
    arrived(weight_in)
    source = wsend[...].astype(f32)
    for b in range(1, B_):
        source = source + wrecv[b].astype(f32)
    gws_ref[...] = source
    for copy in started:
        copy.wait_send()


def write_out(*refs):
    sems = refs[-1]
    copies = [
        pltpu.make_async_copy(refs[i], refs[8 + i], sems.at[i]) for i in range(8)]
    for copy in copies:
        copy.start()
    for copy in copies:
        copy.wait()


def fused_on_device(
    patches, chans,
    grid_latent, mesh_latent, w_source, w_dest, w_out, edge_bias, norm_gain,
    edge_source, edge_patch, edge_node, cotangent,
):
    G, W = grid_latent.shape
    M = mesh_latent.shape[0]
    L = w_source.shape[0]
    E = edge_source.shape[0]
    N = patches * M
    near = 2 if patches % 2 == 0 else 1
    far = patches // near
    vmem = pl.BlockSpec(memory_space=pltpu.VMEM)
    hbm = pl.BlockSpec(memory_space=pltpu.HBM)
    sds = jax.ShapeDtypeStruct

    def buf(*shape, dtype=bf16):
        return pltpu.VMEM(shape, dtype)

    def sems(*shape):
        return [pltpu.SemaphoreType.DMA(shape), pltpu.SemaphoreType.DMA(shape)]

    nodes = buf(patches, M, W)
    outs = pl.pallas_call(
        functools.partial(fused_kernel, patches, chans, near),
        out_shape=(
            sds((M, W), bf16), sds((G, W), bf16), sds((M, W), bf16),
            sds((L, W), f32), sds((L, W), f32), sds((L, W), f32),
            sds((1, W), f32), sds((1, W), f32),
        ),
        in_specs=[hbm] * 11,
        out_specs=(vmem,) * 8,
        scratch_shapes=[
            buf(L, W), buf(W, L), buf(L, W), buf(W, L), buf(L, L),
            buf(chans, far, G, W), buf(chans, M, W), buf(chans, M, W), buf(chans, 8, W, dtype=f32),
            buf(1, W, dtype=f32), buf(1, W, dtype=f32), buf(far, 1, 3 * E, dtype=jnp.int32),
            nodes, nodes, nodes, nodes, nodes, nodes, buf(chans, M, W), buf(chans, M, W, dtype=f32),
            buf(chans, M, W), nodes, nodes, buf(chans, G, W), buf(chans, M, W),
            buf(2, chans, patches, M, W), buf(chans, 2, W, N),
            buf(far, E, G + N), buf(far, G, E), buf(N, E), buf(far, E, W, dtype=f32),
            buf(L, far * G), buf(far * G, W), buf(L, W), buf(near, L, W),
            buf(8, W, dtype=f32), buf(patches, 8, W, dtype=f32),
            pltpu.SemaphoreType.DMA((13,)),
            *sems(7, chans), *sems(9, patches), *sems(6, far), *sems(3, chans + 1), *sems(5, near),
        ],
        compiler_params=pltpu.CompilerParams(
            collective_id=0, has_side_effects=True, vmem_limit_bytes=60 * 1024 * 1024),
    )(
        grid_latent, mesh_latent, cotangent, edge_bias.reshape(1, W), norm_gain.reshape(1, W),
        edge_source.reshape(1, E), edge_patch.reshape(1, E), edge_node.reshape(1, E),
        w_source, w_dest, w_out,
    )
    outs = pl.pallas_call(
        write_out,
        out_shape=tuple(sds(out.shape, out.dtype) for out in outs),
        in_specs=[vmem] * 8,
        out_specs=(hbm,) * 8,
        scratch_shapes=[pltpu.SemaphoreType.DMA((8,))],
    )(*outs)
    return outs[:6] + (outs[6].reshape(W), outs[7].reshape(W))


def device_program(mesh):
    patches, chans = mesh.shape["patch"], mesh.shape["chan"]
    if patches <= 16:
        return functools.partial(fused_on_device, patches, chans)
    return on_device


def solution(mesh):
    placed = (
        P("patch", "chan"),
        P("patch", "chan"),
        P(),
        P(),
        P(),
        P("chan"),
        P("chan"),
        P("patch"),
        P("patch", None),
        P("patch"),
        P("patch", "chan"),
    )
    return jax.shard_map(
        device_program(mesh),
        mesh=mesh,
        in_specs=placed,
        out_specs=(
            P("patch", "chan"),
            P("patch", "chan"),
            P("patch", "chan"),
            P(None, "chan"),
            P(None, "chan"),
            P(None, "chan"),
            P("chan"),
            P("chan"),
        ),
        check_vma=False,
    )
```

```python
import functools
import math

import jax
import jax.numpy as jnp
from jax import lax
from jax.experimental import pallas as pl
from jax.experimental.pallas import tpu as pltpu
from jax.sharding import PartitionSpec as P

norm_eps = 1e-05


def slot_ranks(dest_patch, patches):
    edge_count = dest_patch.shape[0]
    block_width = math.gcd(edge_count, 128)
    onehot = (
        dest_patch.reshape(edge_count // block_width, block_width)[:, :, None]
        == jnp.arange(patches, dtype=jnp.int32)[None, None, :]
    ).astype(jnp.float32)
    strict_lower = (jnp.arange(block_width)[:, None] > jnp.arange(block_width)[None, :]).astype(
        jnp.float32
    )
    within = jnp.einsum("ij,bjp->bip", strict_lower, onehot, precision=lax.Precision.HIGHEST)
    counts = jnp.sum(onehot, axis=1)
    blocks = jnp.arange(counts.shape[0])
    earlier = (blocks[:, None] > blocks[None, :]).astype(jnp.float32)
    before = jnp.dot(earlier, counts, precision=lax.Precision.HIGHEST)
    position = jnp.sum((within + before[:, None, :]) * onehot, axis=2)
    return position.reshape(edge_count).astype(jnp.int32)


def contract_rows(left, right):
    return lax.dot_general(
        left, right, (((0,), (0,)), ((), ())), preferred_element_type=jnp.float32
    )


def contract_cols(left, right):
    return lax.dot_general(
        left, right, (((1,), (1,)), ((), ())), preferred_element_type=jnp.float32
    )


def on_device(
    grid_latent,
    mesh_latent,
    w_source,
    w_dest,
    w_out,
    edge_bias,
    norm_gain,
    edge_source,
    edge_patch,
    edge_node,
    cotangent,
):
    patches = lax.axis_size("patch")
    slice_width = grid_latent.shape[1]
    latent_width = w_source.shape[0]
    offset = lax.axis_index("chan") * slice_width
    grid_count = grid_latent.shape[0]
    mesh_count = mesh_latent.shape[0]
    edge_count = edge_source.shape[0]
    capacity = max(2, 2 * edge_count // patches)
    slots = patches * capacity
    dest_patch = edge_patch[:, 0]
    slot_index = dest_patch * capacity + slot_ranks(dest_patch, patches)
    grid_full = lax.all_gather(grid_latent, "chan", axis=1, tiled=True)
    mesh_full = lax.all_gather(mesh_latent, "chan", axis=1, tiled=True)
    source_cols = lax.dynamic_slice_in_dim(w_source, offset, slice_width, 1)
    dest_cols = lax.dynamic_slice_in_dim(w_dest, offset, slice_width, 1)
    out_cols = lax.dynamic_slice_in_dim(w_out, offset, slice_width, 1)
    mesh_proj = jnp.dot(mesh_full, dest_cols, preferred_element_type=jnp.float32)
    empty_rows = jnp.zeros((slots, slice_width), jnp.bfloat16)
    projected = jnp.dot(grid_full, source_cols, preferred_element_type=jnp.float32).astype(
        jnp.bfloat16
    )
    outgoing = empty_rows.at[slot_index].set(projected[edge_source])
    targets = jnp.full((slots,), mesh_count, jnp.int32).at[slot_index].set(edge_node)
    arrived = lax.all_to_all(
        outgoing.reshape(patches, capacity, slice_width),
        "patch",
        split_axis=0,
        concat_axis=0,
        tiled=True,
    )
    landed = lax.all_to_all(
        targets.reshape(patches, capacity), "patch", split_axis=0, concat_axis=0, tiled=True
    )
    edge_values = arrived.reshape(slots, slice_width)
    landed = landed.reshape(slots)
    is_live = landed < mesh_count
    safe_node = jnp.minimum(landed, mesh_count - 1)
    pre_act = edge_values.astype(jnp.float32) + mesh_proj[safe_node] + edge_bias
    message = jnp.where(is_live[:, None], jax.nn.silu(pre_act), 0.0)
    summed = jax.ops.segment_sum(message, safe_node, num_segments=mesh_count).astype(jnp.bfloat16)
    summed_full = lax.all_gather(summed, "chan", axis=1, tiled=True)
    mixed = jnp.dot(summed_full, out_cols, preferred_element_type=jnp.float32)
    row_total, row_square = lax.psum(
        (jnp.sum(mixed, axis=1), jnp.sum(mixed * mixed, axis=1)), "chan"
    )
    row_mean = row_total / latent_width
    row_var = jnp.maximum(row_square / latent_width - row_mean * row_mean, 0.0)
    inv_scale = lax.rsqrt(row_var + norm_eps)
    normed = (mixed - row_mean[:, None]) * inv_scale[:, None]
    updated = (mesh_latent.astype(jnp.float32) + normed * norm_gain).astype(jnp.bfloat16)
    cotan_full = cotangent.astype(jnp.float32)
    gain_local = jnp.sum(cotan_full * normed, axis=0)
    scaled = cotan_full * norm_gain
    scaled_total, cross_total = lax.psum(
        (jnp.sum(scaled, axis=1), jnp.sum(scaled * normed, axis=1)), "chan"
    )
    grad_mixed = (
        (
            scaled
            - scaled_total[:, None] / latent_width
            - normed * (cross_total[:, None] / latent_width)
        )
        * inv_scale[:, None]
    ).astype(jnp.bfloat16)
    out_local = contract_rows(summed_full, grad_mixed)
    grad_full = lax.all_gather(grad_mixed, "chan", axis=1, tiled=True)
    grad_summed = contract_cols(grad_full, lax.dynamic_slice_in_dim(w_out, offset, slice_width, 0))
    sigmoid_val = jax.nn.sigmoid(pre_act)
    silu_slope = sigmoid_val * (1.0 + pre_act * (1.0 - sigmoid_val))
    grad_pre = jnp.where(is_live[:, None], grad_summed[safe_node] * silu_slope, 0.0).astype(
        jnp.bfloat16
    )
    grad_edges = grad_pre.astype(jnp.float32)
    bias_local = jnp.sum(grad_edges, axis=0)
    grad_mesh_proj = jax.ops.segment_sum(grad_edges, safe_node, num_segments=mesh_count).astype(
        jnp.bfloat16
    )
    returned = lax.all_to_all(
        grad_pre.reshape(patches, capacity, slice_width),
        "patch",
        split_axis=0,
        concat_axis=0,
        tiled=True,
    )
    per_edge = returned.reshape(slots, slice_width)[slot_index]
    grad_projected = jax.ops.segment_sum(
        per_edge.astype(jnp.float32), edge_source, num_segments=grid_count
    ).astype(jnp.bfloat16)
    dest_local = contract_rows(mesh_full, grad_mesh_proj)
    source_local = contract_rows(grid_full, grad_projected)
    node_full = lax.all_gather(grad_mesh_proj, "chan", axis=1, tiled=True)
    grad_mesh = (
        cotan_full
        + contract_cols(node_full, lax.dynamic_slice_in_dim(w_dest, offset, slice_width, 0))
    ).astype(jnp.bfloat16)
    source_full = lax.all_gather(grad_projected, "chan", axis=1, tiled=True)
    grad_grid = contract_cols(
        source_full, lax.dynamic_slice_in_dim(w_source, offset, slice_width, 0)
    ).astype(jnp.bfloat16)
    grad_w_source, grad_w_dest, grad_w_out, grad_bias, grad_gain = lax.psum(
        (source_local, dest_local, out_local, bias_local, gain_local), "patch"
    )
    return (
        updated,
        grad_grid,
        grad_mesh,
        grad_w_source,
        grad_w_dest,
        grad_w_out,
        grad_bias,
        grad_gain,
    )


MESH = pl.DeviceIdType.MESH
f32, bf16 = jnp.float32, jnp.bfloat16


def fused_kernel(
    P_, C_, B_,
    grid_hbm, mesh_hbm, cot_hbm, bias_hbm, gain_hbm, src_hbm, patch_hbm, node_hbm,
    ws_hbm, wd_hbm, wo_hbm,
    upd_ref, ggrid_ref, gmesh_ref, gws_ref, gwd_ref, gwo_ref, gbias_ref, ggain_ref,
    ws_col, ws_row, wd_col, wd_row, wo,
    gridz, meshb, cotb, gainb, bias_ref, gain_ref, ends,
    mp, ps, pr, qs, qr, qn, sm, nrm, gm, gs, gmn, gp, gmp, ns, nt,
    ends_h, src_t, dst_t, slope, grid_t, gpz, wsend, wrecv, bsend, brecv,
    w_sem, c_send, c_recv, p_send, p_recv, z_send, z_recv, s_send, s_recv, x_send, x_recv,
):
    me_p, me_c = lax.axis_index("patch"), lax.axis_index("chan")
    G, W = grid_hbm.shape
    M = mesh_hbm.shape[0]
    L = C_ * W
    E = src_hbm.shape[1]
    N = P_ * M
    H_ = P_ // B_
    lo, hi = lax.rem(me_p, B_), me_p // B_
    started = []

    def within(x, n):
        return jnp.where(x >= n, x - n, x)

    aheads = [within(hi + k % H_, H_) * B_ + within(lo + k // H_, B_) for k in range(P_)]
    behinds = [within(hi + (H_ - k % H_) % H_, H_) * B_ + within(lo + (B_ - k // H_) % B_, B_) for k in range(P_)]
    chans = [within(me_c + j, C_) for j in range(C_)]

    barrier = pltpu.get_barrier_semaphore()
    for k in range(1, P_):
        pl.semaphore_signal(barrier, inc=1, device_id=(aheads[k], me_c), device_id_type=MESH)
    for j in range(1, C_):
        pl.semaphore_signal(barrier, inc=1, device_id=(me_p, chans[j]), device_id_type=MESH)

    cols = pl.ds(pl.multiple_of(me_c * W, W), W)
    fills = [
        pltpu.make_async_copy(src, dst, w_sem.at[5 + i]) for i, (src, dst) in enumerate((
            (mesh_hbm, meshb.at[me_c]), (grid_hbm, gridz.at[me_c, 0]), (cot_hbm, cotb.at[me_c]),
            (gain_hbm, gain_ref), (bias_hbm, bias_ref), (src_hbm, ends.at[0, :, pl.ds(0, E)]),
            (patch_hbm, ends.at[0, :, pl.ds(E, E)]), (node_hbm, ends.at[0, :, pl.ds(2 * E, E)])))]
    loads = [
        pltpu.make_async_copy(wd_hbm.at[:, cols], wd_col, w_sem.at[0]),
        pltpu.make_async_copy(ws_hbm.at[:, cols], ws_col, w_sem.at[1]),
        pltpu.make_async_copy(wo_hbm, wo, w_sem.at[2]),
        pltpu.make_async_copy(wd_hbm.at[cols, :], wd_row, w_sem.at[3]),
        pltpu.make_async_copy(ws_hbm.at[cols, :], ws_row, w_sem.at[4]),
    ]
    for load in fills + loads:
        load.start()

    def remote(src, dst, send_sem, recv_sem, to):
        copy = pltpu.make_async_remote_copy(
            src_ref=src, dst_ref=dst, send_sem=send_sem, recv_sem=recv_sem,
            device_id=to, device_id_type=MESH)
        copy.start()
        started.append(copy)
        return copy

    def chan_gather(phase, src, buf):
        return [
            remote(src, buf.at[me_c], c_send.at[phase, j], c_recv.at[phase, j],
                   (me_p, chans[j]))
            for j in range(1, C_)]

    def patch_gather(phase, src, slot):
        return [
            remote(src, slot(k), p_send.at[phase, k], p_recv.at[phase, k], (aheads[k], me_c))
            for k in range(1, P_)]

    def patch_scatter(phase, block, buf):
        return [
            remote(block(k), buf.at[k], p_send.at[phase, k], p_recv.at[phase, k], (behinds[k], me_c))
            for k in range(1, P_)]

    def line_gather(phase, slot):
        return [
            remote(slot(0), slot(h), z_send.at[phase, h], z_recv.at[phase, h], (aheads[h], me_c))
            for h in range(1, H_)]

    def beside(phase, view):
        return [
            remote(view(0), view(b), x_send.at[phase, b], x_recv.at[phase, b], (aheads[b * H_], me_c))
            for b in range(1, B_)]

    even = C_ % 2 == 0
    twin = me_c + 1 - 2 * lax.rem(me_c, 2)

    def spread(phase, view):
        if not even:
            return [], [
                remote(view(me_c), view(me_c), s_send.at[phase, j], s_recv.at[phase, j],
                       (me_p, chans[j]))
                for j in range(1, C_)]
        near = [remote(view(me_c), view(me_c), s_send.at[phase, 0], s_recv.at[phase, 0], (me_p, twin))]
        across = [
            remote(view(me_c), view(me_c), s_send.at[phase, j], s_recv.at[phase, j],
                   (me_p, chans[2 * j]))
            for j in range(1, C_ // 2)]
        return near, across

    def spread_on(phase, view, across):
        arrived(across)
        if not even:
            return []
        passed = []
        for j in range(1, C_ // 2):
            block = view(chans[C_ - 2 * j])
            passed.append(remote(
                block, block, s_send.at[phase, C_ // 2 + j], s_recv.at[phase, C_ // 2 + j], (me_p, twin)))
        return passed

    def arrived(copies):
        for copy in copies:
            copy.wait_recv()

    def wide(buf):
        return jnp.concatenate([buf[c] for c in range(C_)], axis=1)

    def dot(a, b):
        return lax.dot_general(a, b, (((1,), (0,)), ((), ())), preferred_element_type=f32)

    def onehot_of(mask):
        return jnp.where(mask, 1.0, 0.0).astype(bf16)

    def flat(buf):
        return buf[...].reshape(N, W)

    def band_ends(h):
        row = ends[h]
        patch = row[:, E:2 * E]
        line = jnp.zeros_like(patch)
        for z in range(1, H_):
            line = line + jnp.where(patch >= z * B_, 1, 0)
        side = lo - (patch - line * B_)
        side = jnp.where(side < 0, side + B_, side)
        line = hi - line
        line = jnp.where(line < 0, line + H_, line)
        return row[:, :E], (side * H_ + line) * M + row[:, 2 * E:]

    def band_onehots(h):
        src, dst = band_ends(h)
        down = jnp.transpose(jnp.broadcast_to(jnp.concatenate([src, dst], axis=1), (128, 2 * E)))
        lane = lax.broadcasted_iota(jnp.int32, (E, 128), 1)
        for b in range(0, G, 128):
            ends_h[h, :, b:b + 128] = onehot_of(down[:E] == lane + b)
        for b in range(0, N, 128):
            ends_h[h, :, G + b:G + b + 128] = onehot_of(down[E:] == lane + b)
        src_t[h] = onehot_of(lax.broadcasted_iota(jnp.int32, (G, E), 0) == src)

    def band_full(h):
        return jnp.concatenate([gridz[c, h] for c in range(C_)], axis=1)

    def sigmoid(pre):
        return 1.0 / (1.0 + jnp.exp(-pre))

    def silu_slope(pre, sig):
        return sig * (1.0 + pre * (1.0 - sig))

    fills[0].wait()
    pl.semaphore_wait(barrier, P_ + C_ - 2)
    mesh_in = chan_gather(0, meshb.at[me_c], meshb)
    for fill in fills[1:]:
        fill.wait()
    grid_in = chan_gather(1, gridz.at[me_c, 0], gridz.at[:, 0])
    ends_in = line_gather(1, lambda h: ends.at[h])
    gainb[me_c] = jnp.broadcast_to(gain_ref[...], gainb.shape[1:])
    ns[0, me_c, 0] = meshb[me_c]
    nodes_line = line_gather(2, lambda h: ns.at[0, me_c, h])
    line_in = line_gather(0, lambda h: gridz.at[me_c, h, pl.ds(0, 5 * G // 16)])

    loads[0].wait()
    arrived(mesh_in)
    mp[0] = (dot(wide(meshb), wd_col[...]) + bias_ref[...]).astype(bf16)
    mp_in = patch_gather(0, mp.at[0], lambda k: mp.at[k])
    line_in += line_gather(3, lambda h: gridz.at[me_c, h, pl.ds(5 * G // 16, 11 * G // 16)])
    cot_in = chan_gather(2, cotb.at[me_c], cotb)
    gain_in = chan_gather(3, gainb.at[me_c], gainb)

    band_onehots(0)
    dst_t[...] = onehot_of(lax.broadcasted_iota(jnp.int32, (N, E), 0) == band_ends(0)[1])
    loads[1].wait()
    arrived(grid_in)
    projected = dot(band_full(0), ws_col[...]).astype(bf16)
    sender = dot(ends_h[0, :, :G], projected)
    arrived(nodes_line)
    nodes_in = beside(2, lambda b: ns.at[0, me_c, pl.ds(b * H_, H_)])

    arrived(mp_in)
    pre = sender + dot(ends_h[0, :, G:], flat(mp))
    sig = sigmoid(pre)
    part = dot(dst_t[...], (pre * sig).astype(bf16))
    ps[...] = part.astype(bf16).reshape(P_, M, W)
    part_in = patch_scatter(1, lambda k: ps.at[k], pr)
    own_slope = silu_slope(pre, sig)
    slope[0] = own_slope
    turned = dot(dst_t[...], own_slope.astype(bf16))
    qs[...] = turned.astype(bf16).reshape(P_, M, W)
    turned_side = [
        remote(qs.at[pl.ds(b * H_, H_)], qr.at[pl.ds(b * H_, H_)], x_send.at[3, b], x_recv.at[3, b],
               (behinds[b * H_], me_c))
        for b in range(1, B_)]
    total = part[:M]
    line_slopes = turned[:H_ * M].reshape(H_, M, W)

    arrived(ends_in)

    def other_onehots(h, carry):
        band_onehots(h)
        return carry

    lax.fori_loop(1, H_, other_onehots, 0)
    grid_t[:, 0:G] = jnp.transpose(band_full(0))
    arrived(line_in)
    bands = lambda c: gridz.at[c, pl.ds(1, H_ - 1)]
    band_near, band_across = spread(0, bands)

    arrived(part_in)
    for k in range(1, P_):
        total = total + pr[k].astype(f32)
    sm[me_c] = total.astype(bf16)
    sm_in = chan_gather(4, sm.at[me_c], sm)
    ns[1, me_c, 0] = total.astype(bf16)
    sums_in = patch_gather(4, sm.at[me_c], lambda k: ns.at[1, me_c, k])
    arrived(turned_side)
    for b in range(1, B_):
        line_slopes = line_slopes + qr[b * H_:(b + 1) * H_].astype(f32)
    qs[0:H_] = line_slopes.astype(bf16)
    turned_in = [
        remote(qs.at[h], qr.at[h], z_send.at[4, h], z_recv.at[4, h], (behinds[h], me_c))
        for h in range(1, H_)]
    arrived(nodes_in)
    nodes = lambda c: ns.at[0, c]
    nodes_near, nodes_across = spread(1, nodes)
    loads[2].wait()
    arrived(cot_in)
    arrived(gain_in)
    gain_full = jnp.concatenate([gainb[c][0:1] for c in range(C_)], axis=1)
    scaled = wide(cotb).astype(f32) * gain_full
    scaled_mean = jnp.sum(scaled, axis=1, keepdims=True) / L
    arrived(sm_in)
    mixed = dot(wide(sm), wo[...])
    mean = jnp.sum(mixed, axis=1, keepdims=True) / L
    centred = mixed - mean
    var = jnp.sum(centred * centred, axis=1, keepdims=True) / L
    inv = lax.rsqrt(var + norm_eps)
    normed = centred * inv
    cross_mean = jnp.sum(scaled * normed, axis=1, keepdims=True) / L
    grad_mixed = ((scaled - scaled_mean - normed * cross_mean) * inv).astype(bf16)
    grad_summed = contract_cols(grad_mixed, wo[cols, :])
    gs[0] = grad_summed.astype(bf16)
    gs_in = patch_gather(6, gs.at[0], lambda k: gs.at[k])

    arrived(turned_in)
    slope_total = line_slopes[0]
    for h in range(1, H_):
        slope_total = slope_total + qr[h].astype(f32)
    grad_nodes = grad_summed * slope_total
    gmp[me_c] = grad_nodes.astype(bf16)
    gmp_in = chan_gather(6, gmp.at[me_c], gmp)
    band_passed = spread_on(0, bands, band_across)
    for c in range(C_):
        nrm[c] = normed[:, c * W:(c + 1) * W]
        gm[c] = grad_mixed[:, c * W:(c + 1) * W]
    gmn[0] = gm[me_c]
    own_normed = nrm[me_c]
    cot_own = cotb[me_c].astype(f32)
    bsend[...] = jnp.concatenate(
        [jnp.sum(grad_nodes, axis=0, keepdims=True),
         jnp.sum(cot_own * own_normed, axis=0, keepdims=True), jnp.zeros((6, W), f32)], axis=0)
    small_in = patch_gather(8, bsend, lambda k: brecv.at[k])
    upd_ref[...] = (meshb[me_c].astype(f32) + own_normed * gain_ref[...]).astype(bf16)

    gmn_in = patch_gather(7, gmn.at[0], lambda k: gmn.at[k])
    qn[0] = grad_nodes.astype(bf16)
    qn_in = patch_gather(5, qn.at[0], lambda k: qn.at[k])
    arrived(sums_in)
    sums = lambda c: ns.at[1, c]
    sums_near, sums_across = spread(2, sums)

    arrived(band_near)
    arrived(band_passed)

    def other_slopes(h, carry):
        full = band_full(h)
        grid_t[:, pl.ds(pl.multiple_of(h * G, G), G)] = jnp.transpose(full)
        pre = dot(ends_h[h, :, :G], dot(full, ws_col[...]).astype(bf16)) + dot(ends_h[h, :, G:], flat(mp))
        slope[h] = silu_slope(pre, sigmoid(pre))
        return carry

    lax.fori_loop(1, H_, other_slopes, 0)
    nodes_passed = spread_on(1, nodes, nodes_across)
    loads[3].wait()
    loads[4].wait()
    arrived(gmp_in)
    gmesh_ref[...] = (cot_own + contract_cols(wide(gmp), wd_row[...])).astype(bf16)

    def turn(i, c):
        nt[c, i] = jnp.transpose(ns[i, c].reshape(N, W))

    turn(1, me_c)
    arrived(nodes_near)
    arrived(nodes_passed)
    for c in range(C_):
        turn(0, c)
    if even:
        arrived(sums_near)
        turn(1, twin)

    def band_grad(h):
        grad_pre = (dot(ends_h[h, :, G:], flat(gs)) * slope[h]).astype(bf16)
        return dot(src_t[h], grad_pre).astype(bf16)

    arrived(gs_in)
    grad_projected = band_grad(0)
    gp[me_c] = grad_projected
    gp_in = chan_gather(5, gp.at[me_c], gp)
    gpz[0:G] = grad_projected
    for h in range(1, H_):
        gpz[h * G:(h + 1) * G] = band_grad(h)
    weight_in = []
    half = L // 2
    for i in range(2):
        piece = pl.ds(i * half, half)
        wsend[piece] = dot(grid_t[piece, :], gpz[...]).astype(bf16)
        weight_in += [
            remote(wsend.at[piece], wrecv.at[b, piece], x_send.at[i, b], x_recv.at[i, b],
                   (aheads[b * H_], me_c))
            for b in range(1, B_)]

    sums_passed = spread_on(2, sums, sums_across)
    arrived(sums_passed)
    for j in range(1, C_ // 2 if even else C_):
        turn(1, chans[C_ - (2 * j if even else j)])
    if even:
        for j in range(1, C_ // 2):
            turn(1, lax.rem(twin + C_ - 2 * j, C_))
    arrived(gmn_in)
    for c in range(C_):
        gwo_ref[c * W:(c + 1) * W, :] = dot(nt[c, 1], flat(gmn))
    arrived(qn_in)
    grad_nodes_all = flat(qn)
    for c in range(C_):
        gwd_ref[c * W:(c + 1) * W, :] = dot(nt[c, 0], grad_nodes_all)
    arrived(small_in)
    small = bsend[...]
    for k in range(1, P_):
        small = small + brecv[k]
    gbias_ref[...] = small[0:1]
    ggain_ref[...] = small[1:2]
    arrived(gp_in)
    ggrid_ref[...] = contract_cols(wide(gp), ws_row[...]).astype(bf16)
    arrived(weight_in)
    source = wsend[...].astype(f32)
    for b in range(1, B_):
        source = source + wrecv[b].astype(f32)
    gws_ref[...] = source
    for copy in started:
        copy.wait_send()


def write_out(*refs):
    sems = refs[-1]
    copies = [
        pltpu.make_async_copy(refs[i], refs[8 + i], sems.at[i]) for i in range(8)]
    for copy in copies:
        copy.start()
    for copy in copies:
        copy.wait()


def fused_on_device(
    patches, chans,
    grid_latent, mesh_latent, w_source, w_dest, w_out, edge_bias, norm_gain,
    edge_source, edge_patch, edge_node, cotangent,
):
    G, W = grid_latent.shape
    M = mesh_latent.shape[0]
    L = w_source.shape[0]
    E = edge_source.shape[0]
    N = patches * M
    near = 2 if patches % 2 == 0 else 1
    far = patches // near
    vmem = pl.BlockSpec(memory_space=pltpu.VMEM)
    hbm = pl.BlockSpec(memory_space=pltpu.HBM)
    sds = jax.ShapeDtypeStruct

    def buf(*shape, dtype=bf16):
        return pltpu.VMEM(shape, dtype)

    def sems(*shape):
        return [pltpu.SemaphoreType.DMA(shape), pltpu.SemaphoreType.DMA(shape)]

    nodes = buf(patches, M, W)
    outs = pl.pallas_call(
        functools.partial(fused_kernel, patches, chans, near),
        out_shape=(
            sds((M, W), bf16), sds((G, W), bf16), sds((M, W), bf16),
            sds((L, W), f32), sds((L, W), f32), sds((L, W), f32),
            sds((1, W), f32), sds((1, W), f32),
        ),
        in_specs=[hbm] * 11,
        out_specs=(vmem,) * 8,
        scratch_shapes=[
            buf(L, W), buf(W, L), buf(L, W), buf(W, L), buf(L, L),
            buf(chans, far, G, W), buf(chans, M, W), buf(chans, M, W), buf(chans, 8, W, dtype=f32),
            buf(1, W, dtype=f32), buf(1, W, dtype=f32), buf(far, 1, 3 * E, dtype=jnp.int32),
            nodes, nodes, nodes, nodes, nodes, nodes, buf(chans, M, W), buf(chans, M, W, dtype=f32),
            buf(chans, M, W), nodes, nodes, buf(chans, G, W), buf(chans, M, W),
            buf(2, chans, patches, M, W), buf(chans, 2, W, N),
            buf(far, E, G + N), buf(far, G, E), buf(N, E), buf(far, E, W, dtype=f32),
            buf(L, far * G), buf(far * G, W), buf(L, W), buf(near, L, W),
            buf(8, W, dtype=f32), buf(patches, 8, W, dtype=f32),
            pltpu.SemaphoreType.DMA((13,)),
            *sems(7, chans), *sems(9, patches), *sems(6, far), *sems(3, chans + 1), *sems(5, near),
        ],
        compiler_params=pltpu.CompilerParams(
            collective_id=0, has_side_effects=True, vmem_limit_bytes=60 * 1024 * 1024),
    )(
        grid_latent, mesh_latent, cotangent, edge_bias.reshape(1, W), norm_gain.reshape(1, W),
        edge_source.reshape(1, E), edge_patch.reshape(1, E), edge_node.reshape(1, E),
        w_source, w_dest, w_out,
    )
    outs = pl.pallas_call(
        write_out,
        out_shape=tuple(sds(out.shape, out.dtype) for out in outs),
        in_specs=[vmem] * 8,
        out_specs=(hbm,) * 8,
        scratch_shapes=[pltpu.SemaphoreType.DMA((8,))],
    )(*outs)
    return outs[:6] + (outs[6].reshape(W), outs[7].reshape(W))


def device_program(mesh):
    patches, chans = mesh.shape["patch"], mesh.shape["chan"]
    if patches <= 16:
        return functools.partial(fused_on_device, patches, chans)
    return on_device


def solution(mesh):
    placed = (
        P("patch", "chan"),
        P("patch", "chan"),
        P(),
        P(),
        P(),
        P("chan"),
        P("chan"),
        P("patch"),
        P("patch", None),
        P("patch"),
        P("patch", "chan"),
    )
    return jax.shard_map(
        device_program(mesh),
        mesh=mesh,
        in_specs=placed,
        out_specs=(
            P("patch", "chan"),
            P("patch", "chan"),
            P("patch", "chan"),
            P(None, "chan"),
            P(None, "chan"),
            P(None, "chan"),
            P("chan"),
            P("chan"),
        ),
        check_vma=False,
    )
```
